256 devices in a mesh: seq: 32 (over y_lo, z, core), fsdp: 8 (over x, y_hi).
Axes of the slice: x: 4, y: 4 (y_hi: 2, y_lo: 2; y = y_hi * 2 + y_lo), z: 8, core: 2. Of those that a mesh axis runs over, the one named last changes fastest.
Arguments:
- tokens: float32 [1, 12288, 3072], P(None, 'seq', 'fsdp'), may hold values from -6 to 6
- block_mask: int32 [16, 6, 6], replicated, may hold values from 0 to 1, as said below
- space_qkv: bfloat16 [3072, 3, 2048], P(None, None, 'fsdp'), may hold values from -0.109375 to 0.109375
- space_out: bfloat16 [2048, 3072], P('fsdp'), may hold values from -0.1875 to 0.1875
- space_mod: float32 [3, 3072], replicated, may hold values from -2 to 3
- time_qkv: bfloat16 [3072, 3, 2048], P(None, None, 'fsdp'), may hold values from -0.109375 to 0.109375
- time_out: bfloat16 [2048, 3072], P('fsdp'), may hold values from -0.1875 to 0.1875
- time_mod: float32 [3, 3072], replicated, may hold values from -2 to 3
Outputs:
- result: float32 [1, 12288, 3072], P(None, 'seq', 'fsdp')
The draws below stay inside these ranges and needn't reach their ends.
Inputs may be any that keep to these rules, and one draw needn't show every extreme that they name: block_mask[f, i, i] = 1 for every frame f and block i.
All inputs are finite; a program needn't handle non-finite values.
Results may differ from the reference program's by a relative error of at most 0.015.
Values may be sent and summed in bfloat16 or wider, within the bound.
No kernel may reach another device: no remote copies, remote signals or barrier semaphores. Data moves between devices by JAX's collectives and lax.ppermute only.
A program may use at most 128 MiB of HBM per device.

```python
import math
import jax
import jax.numpy as jnp
from jax import lax

D = 3072
HD = 128
P_SIZE = 768
BLOCK = 128
VIDEOS = 1
HEADS = 16
F = 16
TOKV = 12288
NB = 6
N_FSDP = 8


def draw_tokens(key, part):
    jitter = jax.random.normal(jax.random.fold_in(key, 11), (VIDEOS, TOKV, D), jnp.float32)
    values = jitter
    return jnp.clip(values, -6.0, 6.0).astype(jnp.float32)


def draw_block_mask(key, part):
    radius = jax.random.randint(jax.random.fold_in(key, 21), (F, NB, 1), 0, NB)
    row_ids = lax.broadcasted_iota(jnp.int32, (F, NB, NB), 1)
    col_ids = lax.broadcasted_iota(jnp.int32, (F, NB, NB), 2)
    return (jnp.abs(row_ids - col_ids) <= radius).astype(jnp.int32)


def draw_modulation(key, salt):
    folded = jax.random.fold_in(key, salt)
    shift_row = jnp.clip(0.5 * jax.random.normal(jax.random.fold_in(folded, 1), (D,), jnp.float32), -2.0, 2.0)
    scale_row = jnp.clip(0.3 * jax.random.normal(jax.random.fold_in(folded, 2), (D,), jnp.float32), -1.0, 1.0)
    gate_row = jax.random.uniform(jax.random.fold_in(folded, 3), (D,), jnp.float32, 0.3, 1.0)
    return jnp.stack([shift_row, scale_row, gate_row]).astype(jnp.float32)


def draw_space_mod(key, part):
    return draw_modulation(key, 31)


def draw_time_mod(key, part):
    return draw_modulation(key, 32)


def raised(entries, own_key, source, target, blocks, factor):
    owner, partner = [(jnp.arange(entries.shape[dim]) // (entries.shape[dim] // blocks)).reshape([-1 if axis == dim else 1 for axis in range(entries.ndim)]) for dim in (source, target)]
    chosen = jax.random.permutation(own_key, blocks)[partner]
    strong = (owner == chosen) | (owner == (partner + blocks // 2) % blocks)
    return jnp.where(strong, factor * entries, entries)


def block_levels(stream_key, dims, cuts, smallest, top_value):
    loudness = 1.0
    for position, parts in cuts:
        steps = jax.random.uniform(jax.random.fold_in(jax.random.fold_in(stream_key, 6), position), (parts,), jnp.float32, smallest / len(cuts), top_value / len(cuts))
        loudness = loudness * jnp.repeat(jnp.exp(steps), dims[position] // parts).reshape((-1,) + (1,) * (len(dims) - 1 - position))
    return loudness


def scatter_about(own_key, dims, deviation, reach, shards=(), dtype=jnp.bfloat16):
    drawn = deviation * jax.random.normal(own_key, dims, jnp.float32)
    if shards:
        drawn = drawn * block_levels(own_key, dims, shards, -0.22, 0.18)
    return jnp.clip(drawn, -reach, reach).astype(dtype)


def heavy_noise(own_key, extent, scale, limit, cuts, heavy, dtype=jnp.bfloat16):
    entries = scale * jax.random.normal(own_key, extent, jnp.float32)
    if cuts:
        entries = entries * block_levels(own_key, extent, cuts, -0.22, 0.18)
    return jnp.clip(raised(entries, jax.random.fold_in(own_key, 3), *heavy), -limit, limit).astype(dtype)


def setup_inputs(seed: int = 0) -> dict:
    arg_keys = jax.random.split(jax.random.key(seed), 9)
    tokens = draw_tokens(jax.random.fold_in(arg_keys[8], 71), 0)
    block_mask = draw_block_mask(jax.random.fold_in(arg_keys[8], 71), 0)
    space_qkv = scatter_about(arg_keys[2], (D, 3, HEADS * HD), D ** -0.5, 0.109375, ((2, 8),))
    space_out = heavy_noise(arg_keys[3], (HEADS * HD, D), (HEADS * HD) ** -0.5, 0.1875, ((0, 8),), (0, 1, 8, 2.0))
    space_mod = draw_space_mod(jax.random.fold_in(arg_keys[8], 71), 0)
    time_qkv = scatter_about(arg_keys[5], (D, 3, HEADS * HD), D ** -0.5, 0.109375, ((2, 8),))
    time_out = heavy_noise(arg_keys[6], (HEADS * HD, D), (HEADS * HD) ** -0.5, 0.1875, ((0, 8),), (0, 1, 8, 2.0))
    time_mod = draw_time_mod(jax.random.fold_in(arg_keys[8], 71), 0)
    return dict(tokens=tokens, block_mask=block_mask, space_qkv=space_qkv, space_out=space_out, space_mod=space_mod, time_qkv=time_qkv, time_out=time_out, time_mod=time_mod)


EPS = 1e-06

def modulate(stream, modulation):
    values = stream.astype(jnp.float32)
    centre = lax.optimization_barrier(jnp.mean(values, axis=-1, keepdims=True))
    centred = values - centre
    variance = lax.optimization_barrier(jnp.mean(centred * centred, axis=-1, keepdims=True))
    normed = centred * lax.rsqrt(variance + EPS)
    return (normed * (1.0 + modulation[1]) + modulation[0]).astype(jnp.bfloat16)

def softmax_rounded(scores, reduce_axis):
    row_max = lax.optimization_barrier(jnp.max(scores, axis=reduce_axis, keepdims=True))
    lifted = jnp.exp(scores - row_max)
    return (lifted / lax.optimization_barrier(jnp.sum(lifted, axis=reduce_axis, keepdims=True))).astype(jnp.bfloat16)

def out_project(attended, weight):
    group_width = attended.shape[1] // N_FSDP
    running = jnp.zeros((attended.shape[0], weight.shape[1]), jnp.float32)
    for member in range(N_FSDP):
        rounded = jnp.dot(attended[:, member * group_width:(member + 1) * group_width], weight[member * group_width:(member + 1) * group_width], preferred_element_type=jnp.float32).astype(jnp.bfloat16)
        running = running + lax.optimization_barrier(rounded).astype(jnp.float32)
    return running

def spatial_attention(packed, block_mask):
    score_scale = 1.0 / math.sqrt(HD)

    def one_frame(inputs):
        packed_frame, mask_frame = inputs
        queries = packed_frame[:, :, 0].astype(jnp.float32)
        keys_all = packed_frame[:, :, 1].astype(jnp.float32)
        values_all = packed_frame[:, :, 2].astype(jnp.float32)
        scores = jnp.einsum('bqhd,bkhd->bhqk', queries, keys_all) * score_scale
        allowed = jnp.repeat(jnp.repeat(mask_frame == 1, BLOCK, axis=0), BLOCK, axis=1)
        scores = jnp.where(allowed[None, None], scores, -jnp.inf)
        weights_bf = softmax_rounded(scores, 3)
        return jnp.einsum('bhqk,bkhd->bqhd', weights_bf.astype(jnp.float32), values_all).astype(jnp.bfloat16)
    framed = jnp.moveaxis(packed, 1, 0)
    attended = lax.map(one_frame, (framed, block_mask))
    return jnp.moveaxis(attended, 0, 1)

def temporal_attention(packed):
    score_scale = 1.0 / math.sqrt(HD)
    queries = packed[:, :, :, 0].astype(jnp.float32)
    keys_all = packed[:, :, :, 1].astype(jnp.float32)
    values_all = packed[:, :, :, 2].astype(jnp.float32)
    scores = jnp.einsum('bfphd,bgphd->bphfg', queries, keys_all) * score_scale
    weights_bf = softmax_rounded(scores, 4)
    return jnp.einsum('bphfg,bgphd->bfphd', weights_bf.astype(jnp.float32), values_all).astype(jnp.bfloat16)

def sublayer_inputs(stream_flat, qkv_weight, modulation):
    normed = modulate(stream_flat, modulation)
    packed = jnp.dot(normed, qkv_weight.reshape(D, -1), preferred_element_type=jnp.float32)
    return packed.astype(jnp.bfloat16).reshape(VIDEOS, F, P_SIZE, 3, HEADS, HD)

def reference(tokens, block_mask, space_qkv, space_out, space_mod, time_qkv, time_out, time_mod):
    heads_width = HEADS * HD
    flat_tokens = tokens.reshape(-1, D).astype(jnp.float32)
    packed = sublayer_inputs(flat_tokens, space_qkv, space_mod)
    attended = spatial_attention(packed, block_mask).reshape(-1, heads_width)
    summed = out_project(attended, space_out)
    stream = flat_tokens + space_mod[2] * summed
    packed_time = sublayer_inputs(stream, time_qkv, time_mod)
    attended_time = temporal_attention(packed_time).reshape(-1, heads_width)
    summed_time = out_project(attended_time, time_out)
    result = stream + time_mod[2] * summed_time
    return result.reshape(VIDEOS, TOKV, D)
```

```python
import functools
import math

import jax
import jax.numpy as jnp
from jax import lax
from jax.experimental import pallas as pl
from jax.experimental.pallas import tpu as pltpu
from jax.sharding import PartitionSpec as P

HD = 128
BLOCK = 128
EPS = 1e-06
SCALE = 1.0 / math.sqrt(HD)
VMEM_LIMIT = 48 * 1024 * 1024
F32 = jnp.float32
BF16 = jnp.bfloat16


def whole(shape):
    return pl.BlockSpec(shape, lambda *_: (0,) * len(shape))


def params():
    return pltpu.CompilerParams(vmem_limit_bytes=VMEM_LIMIT)


def row_stats(parts_ref, mean_ref, rstd_ref):
    parts, rows, width = parts_ref.shape
    total = jnp.zeros((rows, 1), F32)
    for part in range(parts):
        total += jnp.sum(parts_ref[part].astype(F32), axis=1, keepdims=True)
    mean = total / (parts * width)
    spread = jnp.zeros((rows, 1), F32)
    for part in range(parts):
        centred = parts_ref[part].astype(F32) - mean
        spread += jnp.sum(centred * centred, axis=1, keepdims=True)
    mean_ref[...] = mean
    rstd_ref[...] = lax.rsqrt(spread / (parts * width) + EPS)


def modulated(parts_ref, mod_ref, mean_ref, rstd_ref, step, pair):
    mean, rstd = mean_ref[...], rstd_ref[...]
    width = parts_ref.shape[2]
    pieces = []
    for offset in range(pair):
        values = parts_ref[step * pair + offset].astype(F32)
        shift = mod_ref[0:1, offset * width : (offset + 1) * width]
        gain = 1.0 + mod_ref[1:2, offset * width : (offset + 1) * width]
        pieces.append((((values - mean) * rstd) * gain + shift).astype(BF16))
    return jnp.concatenate(pieces, axis=1)


def accumulate_qkv(parts_ref, mod_ref, weight_ref, acc_ref, mean_ref, rstd_ref, pair):
    step = pl.program_id(0)

    @pl.when(step == 0)
    def _():
        row_stats(parts_ref, mean_ref, rstd_ref)

    normed = modulated(parts_ref, mod_ref, mean_ref, rstd_ref, step, pair)
    width = weight_ref.shape[2]
    for part in range(3):
        product = jnp.dot(normed, weight_ref[part], preferred_element_type=F32)
        columns = slice(part * width, (part + 1) * width)

        @pl.when(step == 0)
        def _():
            acc_ref[:, columns] = product

        @pl.when(step > 0)
        def _():
            acc_ref[:, columns] += product


def space_in_kernel(pair, parts_ref, mod_ref, weight_ref, q_ref, kv_ref, acc_ref, mean_ref, rstd_ref):
    accumulate_qkv(parts_ref, mod_ref, weight_ref, acc_ref, mean_ref, rstd_ref, pair)

    @pl.when(pl.program_id(0) == pl.num_programs(0) - 1)
    def _():
        width = q_ref.shape[1]
        q_ref[...] = acc_ref[:, :width].astype(BF16)
        kv_ref[...] = acc_ref[:, width:].astype(BF16)


def space_in(parts, mod, weight):
    count, rows, width = parts.shape
    pair = 2 if count % 2 == 0 else 1
    heads_width = weight.shape[2]
    return pl.pallas_call(
        functools.partial(space_in_kernel, pair),
        grid=(count // pair,),
        in_specs=[
            whole((count, rows, width)),
            pl.BlockSpec((3, pair * width), lambda k: (0, k)),
            pl.BlockSpec((3, pair * width, heads_width), lambda k: (0, k, 0)),
        ],
        out_specs=[whole((rows, heads_width)), whole((rows, 2 * heads_width))],
        out_shape=[
            jax.ShapeDtypeStruct((rows, heads_width), BF16),
            jax.ShapeDtypeStruct((rows, 2 * heads_width), BF16),
        ],
        scratch_shapes=[
            pltpu.VMEM((rows, 3 * heads_width), F32),
            pltpu.VMEM((rows, 1), F32),
            pltpu.VMEM((rows, 1), F32),
        ],
        compiler_params=params(),
        cost_estimate=pl.CostEstimate(
            flops=2 * rows * count * width * 3 * heads_width,
            bytes_accessed=2 * count * width * (rows + 3 * heads_width),
            transcendentals=0,
        ),
        name="space_in",
    )(parts, mod, weight)


def project_out(attended, weight_ref, out_ref):
    blocks, _, width = out_ref.shape
    for block in range(blocks):
        out_ref[block] = jnp.dot(
            attended, weight_ref[:, block * width : (block + 1) * width], preferred_element_type=F32
        ).astype(BF16)


def space_attend_kernel(where_ref, mask_ref, q_ref, own_ref, other_ref, weight_ref, out_ref):
    rows, heads_width = q_ref.shape
    query_blocks = rows // BLOCK
    key_blocks = 2 * query_blocks
    frame, half = where_ref[0], where_ref[1]
    mask_base = (frame * key_blocks + half * query_blocks) * key_blocks
    heads = []
    for head in range(heads_width // HD):
        key_cols = slice(head * HD, (head + 1) * HD)
        value_cols = slice(heads_width + head * HD, heads_width + (head + 1) * HD)
        keys = [own_ref[:, key_cols], other_ref[:, key_cols]]
        values = [own_ref[:, value_cols], other_ref[:, value_cols]]
        pieces = []
        for block in range(query_blocks):
            query = q_ref[block * BLOCK : (block + 1) * BLOCK, key_cols]
            scored = []
            for side in range(2):
                scores = lax.dot_general(
                    query, keys[side], (((1,), (1,)), ((), ())), preferred_element_type=F32
                )
                side_half = half if side == 0 else 1 - half
                for key_block in range(query_blocks):
                    kept = mask_ref[
                        mask_base + block * key_blocks + side_half * query_blocks + key_block
                    ]
                    bias = jnp.where(kept == 1, 0.0, -jnp.inf).astype(F32)
                    scored.append(
                        scores[:, key_block * BLOCK : (key_block + 1) * BLOCK] * SCALE + bias
                    )
            scored = jnp.concatenate(scored, axis=1)
            row_max = jnp.max(scored, axis=1, keepdims=True)
            lifted = jnp.exp(scored - row_max)
            norm = jnp.sum(lifted, axis=1, keepdims=True)
            lifted = lifted.astype(BF16)
            mixed = jnp.dot(lifted[:, :rows], values[0], preferred_element_type=F32)
            mixed += jnp.dot(lifted[:, rows:], values[1], preferred_element_type=F32)
            pieces.append((mixed / norm).astype(BF16))
        heads.append(jnp.concatenate(pieces, axis=0))
    project_out(jnp.concatenate(heads, axis=1), weight_ref, out_ref)


def space_attend(where, mask, queries, own, other, weight, blocks):
    rows, heads_width = queries.shape
    width = weight.shape[1] // blocks
    return pl.pallas_call(
        space_attend_kernel,
        grid_spec=pltpu.PrefetchScalarGridSpec(
            num_scalar_prefetch=2,
            grid=(1,),
            in_specs=[
                whole(queries.shape),
                whole(own.shape),
                whole(other.shape),
                whole(weight.shape),
            ],
            out_specs=whole((blocks, rows, width)),
        ),
        out_shape=jax.ShapeDtypeStruct((blocks, rows, width), BF16),
        compiler_params=params(),
        cost_estimate=pl.CostEstimate(
            flops=2 * rows * heads_width * (4 * rows + weight.shape[1]),
            bytes_accessed=2 * (weight.size + rows * weight.shape[1] + 5 * rows * heads_width),
            transcendentals=2 * rows * rows * heads_width // HD,
        ),
        name="space_attend",
    )(where, mask, queries, own, other, weight)


def join_kernel(where_ref, parts_ref, tokens_ref, mod_ref, stream_ref, sent_ref):
    total = parts_ref[0].astype(F32)
    for part in range(1, parts_ref.shape[0]):
        total += parts_ref[part].astype(F32)
    stream = tokens_ref[...] + mod_ref[2:3, :] * total
    stream_ref[...] = stream
    sent_ref[...] = stream.astype(BF16)


def join(where, parts, tokens, mod):
    count, rows, width = parts.shape
    tile = BLOCK
    return pl.pallas_call(
        join_kernel,
        grid_spec=pltpu.PrefetchScalarGridSpec(
            num_scalar_prefetch=1,
            grid=(rows // tile,),
            in_specs=[
                pl.BlockSpec((count, tile, width), lambda i, w: (0, i, 0)),
                pl.BlockSpec((tile, width), lambda i, w: (i, 0)),
                pl.BlockSpec((3, width), lambda i, w: (0, w[2])),
            ],
            out_specs=[
                pl.BlockSpec((tile, width), lambda i, w: (i, 0)),
                pl.BlockSpec((tile, width), lambda i, w: (i, 0)),
            ],
        ),
        out_shape=[
            jax.ShapeDtypeStruct((rows, width), F32),
            jax.ShapeDtypeStruct((rows, width), BF16),
        ],
        compiler_params=params(),
        name="join",
    )(where, parts, tokens, mod)


def total_kernel(parts_ref, out_ref):
    total = parts_ref[0].astype(F32)
    for part in range(1, parts_ref.shape[0]):
        total += parts_ref[part].astype(F32)
    out_ref[...] = total.astype(BF16)


def total_of(parts):
    count, rows, width = parts.shape
    tile = BLOCK
    return pl.pallas_call(
        total_kernel,
        grid=(rows // tile,),
        in_specs=[pl.BlockSpec((count, tile, width), lambda i: (0, i, 0))],
        out_specs=pl.BlockSpec((tile, width), lambda i: (i, 0)),
        out_shape=jax.ShapeDtypeStruct((rows, width), BF16),
        compiler_params=params(),
        name="total_of",
    )(parts)


def time_kernel(pair, frames, parts_ref, mod_ref, weight_ref, out_weight_ref, out_ref,
                acc_ref, att_ref, mean_ref, rstd_ref):
    accumulate_qkv(parts_ref, mod_ref, weight_ref, acc_ref, mean_ref, rstd_ref, pair)

    @pl.when(pl.program_id(0) == pl.num_programs(0) - 1)
    def _():
        rows, packed_width = acc_ref.shape
        heads_width = packed_width // 3
        places = rows // frames
        group = 8
        span = frames * group
        row_place = lax.broadcasted_iota(jnp.int32, (span, span), 0) % group
        col_place = lax.broadcasted_iota(jnp.int32, (span, span), 1) % group
        bias = jnp.where(row_place == col_place, 0.0, -jnp.inf).astype(F32)
        packed = acc_ref[...].reshape(frames, places, packed_width)
        for start in range(0, places, group):
            chunk = packed[:, start : start + group, :].reshape(span, packed_width).astype(BF16)
            for head in range(heads_width // HD):
                low = head * HD
                query = chunk[:, low : low + HD]
                key = chunk[:, heads_width + low : heads_width + low + HD]
                value = chunk[:, 2 * heads_width + low : 2 * heads_width + low + HD]
                scores = lax.dot_general(
                    query, key, (((1,), (1,)), ((), ())), preferred_element_type=F32
                ) * SCALE + bias
                lifted = jnp.exp(scores - jnp.max(scores, axis=1, keepdims=True))
                norm = jnp.sum(lifted, axis=1, keepdims=True)
                mixed = jnp.dot(lifted.astype(BF16), value, preferred_element_type=F32) / norm
                att_ref[:, start : start + group, low : low + HD] = mixed.reshape(frames, group, HD)
        attended = att_ref[...].reshape(rows, heads_width).astype(BF16)
        project_out(attended, out_weight_ref, out_ref)


def time_layer(parts, mod, weight, out_weight, frames):
    count, rows, width = parts.shape
    pair = 2 if count % 2 == 0 else 1
    heads_width = weight.shape[2]
    return pl.pallas_call(
        functools.partial(time_kernel, pair, frames),
        grid=(count // pair,),
        in_specs=[
            whole((count, rows, width)),
            pl.BlockSpec((3, pair * width), lambda k: (0, k)),
            pl.BlockSpec((3, pair * width, heads_width), lambda k: (0, k, 0)),
            whole(out_weight.shape),
        ],
        out_specs=whole((count, rows, width)),
        out_shape=jax.ShapeDtypeStruct((count, rows, width), BF16),
        scratch_shapes=[
            pltpu.VMEM((rows, 3 * heads_width), F32),
            pltpu.VMEM((frames, rows // frames, heads_width), F32),
            pltpu.VMEM((rows, 1), F32),
            pltpu.VMEM((rows, 1), F32),
        ],
        compiler_params=params(),
        cost_estimate=pl.CostEstimate(
            flops=2 * rows * count * width * 4 * heads_width,
            bytes_accessed=2 * count * width * (2 * rows + 4 * heads_width),
            transcendentals=rows * BLOCK * heads_width // HD,
        ),
        name="time_layer",
    )(parts, mod, weight, out_weight)


def gathered(shard, count):
    copies = jnp.broadcast_to(shard[None], (count,) + shard.shape)
    return lax.all_to_all(copies, "fsdp", split_axis=0, concat_axis=0, tiled=True)


def on_device(tokens, block_mask, space_qkv, space_out, space_mod, time_qkv, time_out, time_mod):
    videos, rows, width = tokens.shape
    parts = lax.axis_size("fsdp")
    seq_count = lax.axis_size("seq")
    frames = seq_count // 2
    places = rows // frames
    seq_index = lax.axis_index("seq")
    where = jnp.stack([seq_index // 2, seq_index % 2, lax.axis_index("fsdp")]).astype(jnp.int32)
    same_half = [[2 * frame + half for frame in range(frames)] for half in range(2)]

    def across_frames(values):
        return lax.all_to_all(
            values.reshape(frames, places, width), "seq", split_axis=0, concat_axis=0, tiled=True,
            axis_index_groups=same_half,
        ).reshape(rows, width)

    def across_parts(values):
        return lax.all_to_all(values, "fsdp", split_axis=0, concat_axis=0, tiled=True)

    local = tokens.reshape(rows, width)
    queries, own = space_in(
        gathered(local.astype(BF16), parts), space_mod, jnp.swapaxes(space_qkv, 0, 1)
    )
    other = lax.ppermute(own, "seq", [(i, i ^ 1) for i in range(seq_count)])
    partial = space_attend(where, block_mask.reshape(-1), queries, own, other, space_out, parts)
    stream, sent = join(where, across_parts(partial), local, space_mod)
    partial_time = time_layer(
        gathered(across_frames(sent), parts), time_mod, jnp.swapaxes(time_qkv, 0, 1), time_out, frames
    )
    returned = across_frames(total_of(across_parts(partial_time)))
    gate = lax.dynamic_slice_in_dim(time_mod[2], lax.axis_index("fsdp") * width, width, 0)
    return (stream + gate * returned.astype(F32)).reshape(tokens.shape)


def solution(mesh):
    placed = (
        P(None, "seq", "fsdp"),
        P(),
        P(None, None, "fsdp"),
        P("fsdp", None),
        P(),
        P(None, None, "fsdp"),
        P("fsdp", None),
        P(),
    )
    return jax.shard_map(
        on_device, mesh=mesh, in_specs=placed, out_specs=P(None, "seq", "fsdp"), check_vma=False
    )
```

```python
import functools
import math

import jax
import jax.numpy as jnp
from jax import lax
from jax.experimental import pallas as pl
from jax.experimental.pallas import tpu as pltpu
from jax.sharding import PartitionSpec as P

HD = 128
BLOCK = 128
EPS = 1e-06
SCALE = 1.0 / math.sqrt(HD)
VMEM_LIMIT = 32 * 1024 * 1024
F32 = jnp.float32
BF16 = jnp.bfloat16
LINES = 16


def whole(shape):
    return pl.BlockSpec(shape, lambda *_: (0,) * len(shape))


def params():
    return pltpu.CompilerParams(vmem_limit_bytes=VMEM_LIMIT)


def spread_columns(columns, rows):
    lane = lax.broadcasted_iota(jnp.int32, (rows, 128), 1)
    table = jnp.zeros((rows, 128), F32)
    for index, column in enumerate(columns):
        table = jnp.where(lane == index, column, table)
    return table


def bf16_terms(values, count):
    terms = []
    for _ in range(count):
        term = values.astype(BF16).astype(F32)
        terms.append(term)
        values = values - term
    return terms


def centre(values):
    mean = jnp.sum(values, axis=1, keepdims=True) / values.shape[1]
    centred = values - mean
    squares = jnp.sum(centred * centred, axis=1, keepdims=True)
    table = spread_columns(bf16_terms(mean, 3) + bf16_terms(squares, 2), values.shape[0])
    return centred.astype(BF16), table


def pack_kernel(where_ref, tokens_ref, space_ref, time_ref, out_ref):
    parts, _, width = out_ref.shape
    rows = tokens_ref.shape[0]
    centred, table = centre(tokens_ref[...])
    stats = jnp.transpose(table)[:8].astype(BF16)
    second = jnp.full(space_ref.shape, where_ref[1], jnp.int32) == 1
    lines = jnp.where(second, time_ref[...].astype(F32), space_ref[...].astype(F32)).astype(BF16)
    for part in range(parts):
        out_ref[part, :rows, :] = centred
        out_ref[part, rows : rows + LINES, :] = lines[:, part * width : (part + 1) * width]
        out_ref[part, rows + LINES :, :] = stats


def pack(where, tokens, space_out, time_out):
    rows, width = tokens.shape
    model_width = space_out.shape[1]
    parts = model_width // width
    line_spec = pl.BlockSpec((LINES, model_width), lambda i, w: (w[0], 0))
    shape = (parts, rows + LINES + 8, width)
    return pl.pallas_call(
        pack_kernel,
        grid_spec=pltpu.PrefetchScalarGridSpec(
            num_scalar_prefetch=1,
            grid=(1,),
            in_specs=[whole(tokens.shape), line_spec, line_spec],
            out_specs=whole(shape),
        ),
        out_shape=jax.ShapeDtypeStruct(shape, BF16),
        compiler_params=params(),
        name="pack",
    )(where, tokens, space_out, time_out)


def repack_kernel(arrived_ref, out_ref):
    parts, _, width = out_ref.shape
    rows = arrived_ref.shape[0]
    stats = jnp.transpose(arrived_ref[:, width:].astype(F32))[:8].astype(BF16)
    for part in range(parts):
        out_ref[part, :rows, :] = arrived_ref[:, :width]
        out_ref[part, rows:, :] = stats


def repack(arrived, parts):
    rows, width = arrived.shape
    shape = (parts, rows + 8, width - 128)
    return pl.pallas_call(
        repack_kernel,
        grid=(1,),
        in_specs=[whole(arrived.shape)],
        out_specs=whole(shape),
        out_shape=jax.ShapeDtypeStruct(shape, BF16),
        compiler_params=params(),
        name="repack",
    )(arrived)


def row_stats(stats_ref, offset_ref, scale_ref, width):
    parts = stats_ref.shape[0]
    means, squares = [], 0.0
    for part in range(parts):
        lines = stats_ref[part].astype(F32)
        means.append(lines[0:1] + lines[1:2] + lines[2:3])
        squares = squares + (lines[3:4] + lines[4:5])
    mean = sum(means) / parts
    offsets = [part_mean - mean for part_mean in means]
    between = sum(offset * offset for offset in offsets) * width
    scale = lax.rsqrt((squares + between) / (parts * width) + EPS)
    rows = mean.shape[1]
    line = lax.broadcasted_iota(jnp.int32, (128, rows), 0)
    table = jnp.zeros((128, rows), F32)
    for index, entry in enumerate(offsets + [scale]):
        table = jnp.where(line == index, entry, table)
    table = jnp.transpose(table)
    for part in range(parts):
        offset_ref[part] = jnp.broadcast_to(table[:, part : part + 1], (rows, 128))
    scale_ref[...] = jnp.broadcast_to(table[:, parts : parts + 1], (rows, 128))


def accumulate_qkv(parts_ref, stats_ref, mod_ref, weight_ref, acc_ref, offset_ref, scale_ref):
    step = pl.program_id(0)
    pair, rows, width = parts_ref.shape

    @pl.when(step == 0)
    def _():
        row_stats(stats_ref, offset_ref, scale_ref, width)

    scale = scale_ref[...]
    pieces = []
    for index in range(pair):
        offset = offset_ref[step * pair + index]
        for start in range(0, width, 128):
            columns = slice(index * width + start, index * width + start + 128)
            values = parts_ref[index, :, start : start + 128].astype(F32)
            shift = mod_ref[0:1, columns]
            gain = 1.0 + mod_ref[1:2, columns]
            pieces.append((((values + offset) * scale) * gain + shift).astype(BF16))
    normed = jnp.concatenate(pieces, axis=1)
    heads_width = weight_ref.shape[2]
    for part in range(3):
        product = jnp.dot(normed, weight_ref[part], preferred_element_type=F32)
        columns = slice(part * heads_width, (part + 1) * heads_width)

        @pl.when(step == 0)
        def _():
            acc_ref[:, columns] = product

        @pl.when(step > 0)
        def _():
            acc_ref[:, columns] += product


def qkv_specs(parts, rows, width, heads_width):
    count, total_rows, _ = parts.shape
    pair = 2 if count % 2 == 0 else 1
    last = total_rows // 8 - 1
    grid = (count // pair,)
    in_specs = [
        pl.BlockSpec((pair, rows, width), lambda k: (k, 0, 0)),
        pl.BlockSpec((count, 8, width), lambda k: (0, last, 0)),
        pl.BlockSpec((3, pair * width), lambda k: (0, k)),
        pl.BlockSpec((3, pair * width, heads_width), lambda k: (0, k, 0)),
    ]
    scratch = [
        pltpu.VMEM((rows, 3 * heads_width), F32),
        pltpu.VMEM((count, rows, 128), F32),
        pltpu.VMEM((rows, 128), F32),
    ]
    cost = pl.CostEstimate(
        flops=2 * rows * count * width * 3 * heads_width,
        bytes_accessed=2 * count * width * (rows + 3 * heads_width),
        transcendentals=0,
    )
    return grid, in_specs, scratch, cost


def space_in_kernel(parts_ref, stats_ref, mod_ref, weight_ref, q_ref, kv_ref, *scratch):
    accumulate_qkv(parts_ref, stats_ref, mod_ref, weight_ref, *scratch)
    acc_ref = scratch[0]

    @pl.when(pl.program_id(0) == pl.num_programs(0) - 1)
    def _():
        width = q_ref.shape[1]
        q_ref[...] = acc_ref[:, :width].astype(BF16)
        kv_ref[...] = acc_ref[:, width:].astype(BF16)


def space_in(parts, mod, weight, rows):
    width, heads_width = parts.shape[2], weight.shape[2]
    grid, in_specs, scratch, cost = qkv_specs(parts, rows, width, heads_width)
    return pl.pallas_call(
        space_in_kernel,
        grid=grid,
        in_specs=in_specs,
        out_specs=[whole((rows, heads_width)), whole((rows, 2 * heads_width))],
        out_shape=[
            jax.ShapeDtypeStruct((rows, heads_width), BF16),
            jax.ShapeDtypeStruct((rows, 2 * heads_width), BF16),
        ],
        scratch_shapes=scratch,
        compiler_params=params(),
        cost_estimate=cost,
        name="space_in",
    )(parts, parts, mod, weight)


def project_out(attended, weight_ref, out_ref):
    blocks, _, width = out_ref.shape
    for block in range(blocks):
        out_ref[block] = jnp.dot(
            attended, weight_ref[:, block * width : (block + 1) * width], preferred_element_type=F32
        ).astype(BF16)


def space_attend_kernel(where_ref, mask_ref, q_ref, own_ref, other_ref, weight_ref, out_ref):
    rows, heads_width = q_ref.shape
    query_blocks = rows // BLOCK
    key_blocks = 2 * query_blocks
    frame, half = where_ref[0], where_ref[1]
    mask_base = (frame * key_blocks + half * query_blocks) * key_blocks
    heads = []
    for head in range(heads_width // HD):
        key_cols = slice(head * HD, (head + 1) * HD)
        value_cols = slice(heads_width + head * HD, heads_width + (head + 1) * HD)
        keys = [own_ref[:, key_cols], other_ref[:, key_cols]]
        values = [own_ref[:, value_cols], other_ref[:, value_cols]]
        pieces = []
        for block in range(query_blocks):
            query = q_ref[block * BLOCK : (block + 1) * BLOCK, key_cols]
            scored = []
            for side in range(2):
                scores = lax.dot_general(
                    query, keys[side], (((1,), (1,)), ((), ())), preferred_element_type=F32
                )
                side_half = half if side == 0 else 1 - half
                for key_block in range(query_blocks):
                    kept = mask_ref[
                        mask_base + block * key_blocks + side_half * query_blocks + key_block
                    ]
                    bias = jnp.where(kept == 1, 0.0, -jnp.inf).astype(F32)
                    scored.append(
                        scores[:, key_block * BLOCK : (key_block + 1) * BLOCK] * SCALE + bias
                    )
            scored = jnp.concatenate(scored, axis=1)
            row_max = jnp.max(scored, axis=1, keepdims=True)
            lifted = jnp.exp(scored - row_max)
            norm = jnp.sum(lifted, axis=1, keepdims=True)
            lifted = lifted.astype(BF16)
            mixed = jnp.dot(lifted[:, :rows], values[0], preferred_element_type=F32)
            mixed += jnp.dot(lifted[:, rows:], values[1], preferred_element_type=F32)
            pieces.append((mixed / norm).astype(BF16))
        heads.append(jnp.concatenate(pieces, axis=0))
    project_out(jnp.concatenate(heads, axis=1), weight_ref, out_ref)


def space_attend(where, mask, queries, own, other, weight, blocks):
    rows, heads_width = queries.shape
    width = weight.shape[1] // blocks
    return pl.pallas_call(
        space_attend_kernel,
        grid_spec=pltpu.PrefetchScalarGridSpec(
            num_scalar_prefetch=2,
            grid=(1,),
            in_specs=[
                whole(queries.shape),
                whole(own.shape),
                whole(other.shape),
                whole(weight.shape),
            ],
            out_specs=whole((blocks, rows, width)),
        ),
        out_shape=jax.ShapeDtypeStruct((blocks, rows, width), BF16),
        compiler_params=params(),
        cost_estimate=pl.CostEstimate(
            flops=2 * rows * heads_width * (4 * rows + weight.shape[1]),
            bytes_accessed=2 * (weight.size + rows * weight.shape[1] + 5 * rows * heads_width),
            transcendentals=2 * rows * rows * heads_width // HD,
        ),
        name="space_attend",
    )(where, mask, queries, own, other, weight)


def join_kernel(where_ref, parts_ref, tokens_ref, mod_ref, stream_ref, sent_ref):
    total = parts_ref[0].astype(F32)
    for part in range(1, parts_ref.shape[0]):
        total += parts_ref[part].astype(F32)
    stream = tokens_ref[...] + mod_ref[2:3, :] * total
    stream_ref[...] = stream
    centred, table = centre(stream)
    sent_ref[:, : stream.shape[1]] = centred
    sent_ref[:, stream.shape[1] :] = table.astype(BF16)


def join(where, parts, tokens, mod):
    count, rows, width = parts.shape
    tile = BLOCK
    return pl.pallas_call(
        join_kernel,
        grid_spec=pltpu.PrefetchScalarGridSpec(
            num_scalar_prefetch=1,
            grid=(rows // tile,),
            in_specs=[
                pl.BlockSpec((count, tile, width), lambda i, w: (0, i, 0)),
                pl.BlockSpec((tile, width), lambda i, w: (i, 0)),
                pl.BlockSpec((3, width), lambda i, w: (0, w[2])),
            ],
            out_specs=[
                pl.BlockSpec((tile, width), lambda i, w: (i, 0)),
                pl.BlockSpec((tile, width + 128), lambda i, w: (i, 0)),
            ],
        ),
        out_shape=[
            jax.ShapeDtypeStruct((rows, width), F32),
            jax.ShapeDtypeStruct((rows, width + 128), BF16),
        ],
        compiler_params=params(),
        name="join",
    )(where, parts, tokens, mod)


def time_kernel(frames, parts_ref, stats_ref, mod_ref, weight_ref, out_ref, att_ref, *scratch):
    accumulate_qkv(parts_ref, stats_ref, mod_ref, weight_ref, *scratch)
    acc_ref = scratch[0]

    @pl.when(pl.program_id(0) == pl.num_programs(0) - 1)
    def _():
        rows, packed_width = acc_ref.shape
        heads_width = packed_width // 3
        places = rows // frames
        group = 8
        span = frames * group
        row_place = lax.broadcasted_iota(jnp.int32, (span, span), 0) % group
        col_place = lax.broadcasted_iota(jnp.int32, (span, span), 1) % group
        bias = jnp.where(row_place == col_place, 0.0, -jnp.inf).astype(F32)
        packed = acc_ref[...].reshape(frames, places, packed_width)
        for start in range(0, places, group):
            chunk = packed[:, start : start + group, :].reshape(span, packed_width).astype(BF16)
            for head in range(heads_width // HD):
                low = head * HD
                query = chunk[:, low : low + HD]
                key = chunk[:, heads_width + low : heads_width + low + HD]
                value = chunk[:, 2 * heads_width + low : 2 * heads_width + low + HD]
                scores = lax.dot_general(
                    query, key, (((1,), (1,)), ((), ())), preferred_element_type=F32
                ) * SCALE + bias
                lifted = jnp.exp(scores - jnp.max(scores, axis=1, keepdims=True))
                norm = jnp.sum(lifted, axis=1, keepdims=True)
                mixed = jnp.dot(lifted.astype(BF16), value, preferred_element_type=F32) / norm
                att_ref[:, start : start + group, low : low + HD] = mixed.reshape(frames, group, HD)
        out_ref[...] = att_ref[...].reshape(rows, heads_width).astype(BF16)


def time_layer(parts, mod, weight, rows, frames):
    width, heads_width = parts.shape[2], weight.shape[2]
    grid, in_specs, scratch, cost = qkv_specs(parts, rows, width, heads_width)
    return pl.pallas_call(
        functools.partial(time_kernel, frames),
        grid=grid,
        in_specs=in_specs,
        out_specs=whole((rows, heads_width)),
        out_shape=jax.ShapeDtypeStruct((rows, heads_width), BF16),
        scratch_shapes=[pltpu.VMEM((frames, rows // frames, heads_width), F32)] + scratch,
        compiler_params=params(),
        cost_estimate=cost,
        name="time_layer",
    )(parts, parts, mod, weight)


def finish_kernel(where_ref, parts_ref, weight_ref, stream_ref, mod_ref, out_ref):
    count, rows, heads_width = parts_ref.shape
    width = out_ref.shape[1]
    total = jnp.zeros((rows, width), F32)
    for part in range(count):
        lines = weight_ref[:, 0, part].reshape(heads_width, width)
        total += jnp.dot(parts_ref[part], lines, preferred_element_type=F32)
    out_ref[...] = stream_ref[...] + mod_ref[2:3, :] * total


def finish(layer, where, parts, weight, stream, mod):
    count, rows, heads_width = parts.shape
    frames, layers, _, lines, width = weight.shape
    return pl.pallas_call(
        finish_kernel,
        grid_spec=pltpu.PrefetchScalarGridSpec(
            num_scalar_prefetch=1,
            grid=(1,),
            in_specs=[
                whole(parts.shape),
                pl.BlockSpec((frames, 1, count, lines, width), lambda i, w: (0, layer, 0, 0, 0)),
                whole(stream.shape),
                pl.BlockSpec((3, width), lambda i, w: (0, w[2])),
            ],
            out_specs=whole(stream.shape),
        ),
        out_shape=jax.ShapeDtypeStruct(stream.shape, F32),
        compiler_params=params(),
        cost_estimate=pl.CostEstimate(
            flops=2 * rows * count * heads_width * width,
            bytes_accessed=2 * count * heads_width * (rows + width) + 8 * rows * width,
            transcendentals=0,
        ),
        name="finish",
    )(where, parts, weight, stream, mod)


def on_device(tokens, block_mask, space_qkv, space_out, space_mod, time_qkv, time_out, time_mod):
    videos, rows, width = tokens.shape
    parts = lax.axis_size("fsdp")
    seq_count = lax.axis_size("seq")
    frames = seq_count // 2
    seq_index = lax.axis_index("seq")
    where = jnp.stack([seq_index // 2, seq_index % 2, lax.axis_index("fsdp")]).astype(jnp.int32)
    same_half = [[2 * frame + half for frame in range(frames)] for half in range(2)]

    def across_frames(values):
        return lax.all_to_all(
            values.reshape(frames, rows // frames, -1), "seq", split_axis=0, concat_axis=0,
            tiled=True, axis_index_groups=same_half,
        ).reshape(rows, -1)

    def across_parts(values):
        return lax.all_to_all(values, "fsdp", split_axis=0, concat_axis=0, tiled=True)

    local = tokens.reshape(rows, width)
    wide = across_parts(pack(where, local, space_out, time_out))
    lines = lax.all_gather(wide[:, rows : rows + LINES, :], "seq", axis=0, tiled=False)
    lines = lines.reshape(frames, 2, parts, LINES, width)
    queries, own = space_in(wide, space_mod, jnp.swapaxes(space_qkv, 0, 1), rows)
    other = lax.ppermute(own, "seq", [(i, i ^ 1) for i in range(seq_count)])
    partial = space_attend(where, block_mask.reshape(-1), queries, own, other, space_out, parts)
    stream, sent = join(where, across_parts(partial), local, space_mod)
    wide = across_parts(repack(across_frames(sent), parts))
    attended = time_layer(wide, time_mod, jnp.swapaxes(time_qkv, 0, 1), rows, frames)
    attended = across_frames(attended)
    attended = across_parts(jnp.broadcast_to(attended[None], (parts,) + attended.shape))
    return finish(1, where, attended, lines, stream, time_mod).reshape(tokens.shape)


def solution(mesh):
    placed = (
        P(None, "seq", "fsdp"),
        P(),
        P(None, None, "fsdp"),
        P("fsdp", None),
        P(),
        P(None, None, "fsdp"),
        P("fsdp", None),
        P(),
    )
    return jax.shard_map(
        on_device, mesh=mesh, in_specs=placed, out_specs=P(None, "seq", "fsdp"), check_vma=False
    )
```

```python
import functools
import math

import jax
import jax.numpy as jnp
from jax import lax
from jax.experimental import pallas as pl
from jax.experimental.pallas import tpu as pltpu
from jax.sharding import PartitionSpec as P

HD = 128
BLOCK = 128
EPS = 1e-06
SCALE = 1.0 / math.sqrt(HD)
VMEM_LIMIT = 48 * 1024 * 1024
F32 = jnp.float32
BF16 = jnp.bfloat16
STAT_ROWS = 8


def whole(shape):
    return pl.BlockSpec(shape, lambda *_: (0,) * len(shape))


def params():
    return pltpu.CompilerParams(vmem_limit_bytes=VMEM_LIMIT)


def spread_columns(columns, rows):
    lane = lax.broadcasted_iota(jnp.int32, (rows, 128), 1)
    table = jnp.zeros((rows, 128), F32)
    for index, column in enumerate(columns):
        table = jnp.where(lane == index, column, table)
    return table


def bf16_terms(values, count):
    terms = []
    for _ in range(count):
        term = values.astype(BF16).astype(F32)
        terms.append(term)
        values = values - term
    return terms


def centre(values):
    mean = jnp.sum(values, axis=1, keepdims=True) / values.shape[1]
    centred = values - mean
    squares = jnp.sum(centred * centred, axis=1, keepdims=True)
    table = spread_columns(bf16_terms(mean, 3) + bf16_terms(squares, 2), values.shape[0])
    return centred.astype(BF16), table


def pack_kernel(tokens_ref, out_ref):
    parts, total_rows, _ = out_ref.shape
    rows = tokens_ref.shape[0]
    centred, table = centre(tokens_ref[...])
    stats = jnp.transpose(table)[: total_rows - rows].astype(BF16)
    for part in range(parts):
        out_ref[part, :rows, :] = centred
        out_ref[part, rows:, :] = stats


def pack(tokens, parts):
    rows, width = tokens.shape
    shape = (parts, rows + STAT_ROWS, width)
    return pl.pallas_call(
        pack_kernel,
        grid=(1,),
        in_specs=[whole(tokens.shape)],
        out_specs=whole(shape),
        out_shape=jax.ShapeDtypeStruct(shape, BF16),
        compiler_params=params(),
        name="pack",
    )(tokens)


def repack_kernel(arrived_ref, out_ref):
    parts, _, width = out_ref.shape
    rows = arrived_ref.shape[0]
    stats = jnp.transpose(arrived_ref[:, width:].astype(F32))[:STAT_ROWS].astype(BF16)
    for part in range(parts):
        out_ref[part, :rows, :] = arrived_ref[:, :width]
        out_ref[part, rows:, :] = stats


def repack(arrived, parts):
    rows, width = arrived.shape
    shape = (parts, rows + STAT_ROWS, width - 128)
    return pl.pallas_call(
        repack_kernel,
        grid=(1,),
        in_specs=[whole(arrived.shape)],
        out_specs=whole(shape),
        out_shape=jax.ShapeDtypeStruct(shape, BF16),
        compiler_params=params(),
        name="repack",
    )(arrived)


def fold_kernel(mod_ref, weight_ref, folded_ref, offset_ref, shift_ref, gain_sums_ref, shift_sums_ref):
    step, last = pl.program_id(0), pl.num_programs(0) - 1
    _, width, heads_width = weight_ref.shape
    shift = mod_ref[0:1, :]
    gain = 1.0 + mod_ref[1:2, :]
    columns = jnp.transpose(jnp.broadcast_to(gain, (128, width)))
    line = lax.broadcasted_iota(jnp.int32, (16, width), 0)
    lines = jnp.zeros((16, width), F32)
    for index, entry in enumerate(bf16_terms(gain, 2) + bf16_terms(shift, 2)):
        lines = jnp.where(line == index, entry, lines)
    lines = lines.astype(BF16)

    @pl.when(step == 0)
    def _():
        shift_sums_ref[...] = jnp.zeros_like(shift_sums_ref)

    for part in range(3):
        base = part * heads_width
        for start in range(0, heads_width, 128):
            chunk = weight_ref[part, :, start : start + 128].astype(F32)
            folded_ref[part, :, start : start + 128] = (chunk * columns).astype(BF16)
        sums = jnp.dot(lines, weight_ref[part], preferred_element_type=F32)
        gain_sums_ref[pl.ds(step, 1), base : base + heads_width] = sums[0:1] + sums[1:2]
        shift_sums_ref[:, base : base + heads_width] += jnp.broadcast_to(
            sums[2:3] + sums[3:4], (8, heads_width)
        )

    @pl.when(step == last)
    def _():
        high, low = bf16_terms(gain_sums_ref[...], 2)
        rest = jnp.zeros((128 - 3 * high.shape[0], high.shape[1]), F32)
        offset_ref[...] = jnp.concatenate([high, high, low, rest], axis=0).astype(BF16)
        shift_ref[...] = shift_sums_ref[...]


def fold(mod, weight, parts):
    _, model_width, heads_width = weight.shape
    width = model_width // parts
    packed_width = 3 * heads_width
    block = pl.BlockSpec((3, width, heads_width), lambda k: (0, k, 0))
    return pl.pallas_call(
        fold_kernel,
        grid=(parts,),
        in_specs=[pl.BlockSpec((3, width), lambda k: (0, k)), block],
        out_specs=[block, whole((128, packed_width)), whole((8, packed_width))],
        out_shape=[
            jax.ShapeDtypeStruct(weight.shape, BF16),
            jax.ShapeDtypeStruct((128, packed_width), BF16),
            jax.ShapeDtypeStruct((8, packed_width), F32),
        ],
        scratch_shapes=[pltpu.VMEM((parts, packed_width), F32), pltpu.VMEM((8, packed_width), F32)],
        compiler_params=params(),
        cost_estimate=pl.CostEstimate(
            flops=32 * weight.size, bytes_accessed=4 * weight.size, transcendentals=0
        ),
        name="fold",
    )(mod, weight)


def row_table(stats_ref, width):
    parts, _, rows = stats_ref.shape
    line = lax.broadcasted_iota(jnp.int32, (parts, rows), 0)
    means = jnp.zeros((parts, rows), F32)
    squares = 0.0
    for part in range(parts):
        lines = stats_ref[part].astype(F32)
        means = jnp.where(line == part, lines[0:1] + lines[1:2] + lines[2:3], means)
        squares = squares + (lines[3:4] + lines[4:5])
    offsets = means - jnp.sum(means, axis=0, keepdims=True) / parts
    between = jnp.sum(offsets * offsets, axis=0, keepdims=True) * width
    scale = lax.rsqrt((squares + between) / (parts * width) + EPS)
    high, low = bf16_terms(offsets, 2)
    scales = jnp.broadcast_to(scale, (128 - 3 * parts, rows))
    return jnp.transpose(jnp.concatenate([high, low, high, scales], axis=0))


def accumulate_qkv(parts_ref, stats_ref, weight_ref, offset_ref, shift_ref, acc_ref, table_ref):
    step, last = pl.program_id(0), pl.num_programs(0) - 1
    pair, rows, width = parts_ref.shape
    heads_width = weight_ref.shape[2]

    @pl.when(step == 0)
    def _():
        table_ref[...] = row_table(stats_ref, width)

    values = jnp.concatenate([parts_ref[index] for index in range(pair)], axis=1)
    for part in range(3):
        product = jnp.dot(values, weight_ref[part], preferred_element_type=F32)
        columns = slice(part * heads_width, (part + 1) * heads_width)

        @pl.when(step == 0)
        def _():
            terms = jnp.where(
                lax.broadcasted_iota(jnp.int32, (rows, 128), 1) < 3 * stats_ref.shape[0], table_ref[...], 0.0
            ).astype(BF16)
            acc_ref[:, columns] = product + jnp.dot(
                terms, offset_ref[:, columns], preferred_element_type=F32
            )

        @pl.when(step > 0)
        def _():
            acc_ref[:, columns] += product

    @pl.when(step == last)
    def _():
        scale = jnp.broadcast_to(table_ref[:, 127:128], (rows, 128))
        for start in range(0, 3 * heads_width, 128):
            columns = slice(start, start + 128)
            acc_ref[:, columns] = acc_ref[:, columns] * scale + shift_ref[0:1, columns]


def qkv_specs(parts, rows, heads_width):
    count, total_rows, width = parts.shape
    pair = 2 if count % 2 == 0 else 1
    last = total_rows // STAT_ROWS - 1
    grid = (count // pair,)
    in_specs = [
        pl.BlockSpec((pair, rows, width), lambda k: (k, 0, 0)),
        pl.BlockSpec((count, STAT_ROWS, width), lambda k: (0, last, 0)),
        pl.BlockSpec((3, pair * width, heads_width), lambda k: (0, k, 0)),
        whole((128, 3 * heads_width)),
        whole((8, 3 * heads_width)),
    ]
    scratch = [pltpu.VMEM((rows, 3 * heads_width), F32), pltpu.VMEM((rows, 128), F32)]
    cost = pl.CostEstimate(
        flops=2 * rows * count * width * 3 * heads_width,
        bytes_accessed=2 * count * width * (rows + 3 * heads_width),
        transcendentals=0,
    )
    return grid, in_specs, scratch, cost


def space_in_kernel(parts_ref, stats_ref, weight_ref, offset_ref, shift_ref, q_ref, kv_ref,
                    acc_ref, table_ref):
    accumulate_qkv(parts_ref, stats_ref, weight_ref, offset_ref, shift_ref, acc_ref, table_ref)

    @pl.when(pl.program_id(0) == pl.num_programs(0) - 1)
    def _():
        width = q_ref.shape[1]
        q_ref[...] = acc_ref[:, :width].astype(BF16)
        kv_ref[...] = acc_ref[:, width:].astype(BF16)


def space_in(parts, folded, rows):
    heads_width = folded[0].shape[2]
    grid, in_specs, scratch, cost = qkv_specs(parts, rows, heads_width)
    return pl.pallas_call(
        space_in_kernel,
        grid=grid,
        in_specs=in_specs,
        out_specs=[whole((rows, heads_width)), whole((rows, 2 * heads_width))],
        out_shape=[
            jax.ShapeDtypeStruct((rows, heads_width), BF16),
            jax.ShapeDtypeStruct((rows, 2 * heads_width), BF16),
        ],
        scratch_shapes=scratch,
        compiler_params=params(),
        cost_estimate=cost,
        name="space_in",
    )(parts, parts, *folded)


def project_out(attended, weight_ref, out_ref):
    blocks, _, width = out_ref.shape
    for block in range(blocks):
        out_ref[block] = jnp.dot(
            attended, weight_ref[:, block * width : (block + 1) * width], preferred_element_type=F32
        ).astype(BF16)


def space_attend_kernel(where_ref, mask_ref, q_ref, own_ref, other_ref, weight_ref, out_ref):
    rows, heads_width = q_ref.shape
    query_blocks = rows // BLOCK
    key_blocks = 2 * query_blocks
    frame, half = where_ref[0], where_ref[1]
    mask_base = (frame * key_blocks + half * query_blocks) * key_blocks
    heads = []
    for head in range(heads_width // HD):
        key_cols = slice(head * HD, (head + 1) * HD)
        value_cols = slice(heads_width + head * HD, heads_width + (head + 1) * HD)
        keys = [own_ref[:, key_cols], other_ref[:, key_cols]]
        values = [own_ref[:, value_cols], other_ref[:, value_cols]]
        pieces = []
        for block in range(query_blocks):
            query = q_ref[block * BLOCK : (block + 1) * BLOCK, key_cols]
            scored = []
            for side in range(2):
                scores = lax.dot_general(
                    query, keys[side], (((1,), (1,)), ((), ())), preferred_element_type=F32
                )
                side_half = half if side == 0 else 1 - half
                for key_block in range(query_blocks):
                    kept = mask_ref[
                        mask_base + block * key_blocks + side_half * query_blocks + key_block
                    ]
                    bias = jnp.where(kept == 1, 0.0, -jnp.inf).astype(F32)
                    scored.append(
                        scores[:, key_block * BLOCK : (key_block + 1) * BLOCK] * SCALE + bias
                    )
            scored = jnp.concatenate(scored, axis=1)
            row_max = jnp.max(scored, axis=1, keepdims=True)
            lifted = jnp.exp(scored - row_max)
            norm = jnp.sum(lifted, axis=1, keepdims=True)
            lifted = lifted.astype(BF16)
            mixed = jnp.dot(lifted[:, :rows], values[0], preferred_element_type=F32)
            mixed += jnp.dot(lifted[:, rows:], values[1], preferred_element_type=F32)
            pieces.append((mixed / norm).astype(BF16))
        heads.append(jnp.concatenate(pieces, axis=0))
    project_out(jnp.concatenate(heads, axis=1), weight_ref, out_ref)


def space_attend(where, mask, queries, own, other, weight, blocks):
    rows, heads_width = queries.shape
    width = weight.shape[1] // blocks
    return pl.pallas_call(
        space_attend_kernel,
        grid_spec=pltpu.PrefetchScalarGridSpec(
            num_scalar_prefetch=2,
            grid=(1,),
            in_specs=[
                whole(queries.shape),
                whole(own.shape),
                whole(other.shape),
                whole(weight.shape),
            ],
            out_specs=whole((blocks, rows, width)),
        ),
        out_shape=jax.ShapeDtypeStruct((blocks, rows, width), BF16),
        compiler_params=params(),
        cost_estimate=pl.CostEstimate(
            flops=2 * rows * heads_width * (4 * rows + weight.shape[1]),
            bytes_accessed=2 * (weight.size + rows * weight.shape[1] + 5 * rows * heads_width),
            transcendentals=2 * rows * rows * heads_width // HD,
        ),
        name="space_attend",
    )(where, mask, queries, own, other, weight)


def join_kernel(where_ref, parts_ref, tokens_ref, mod_ref, stream_ref, sent_ref):
    total = parts_ref[0].astype(F32)
    for part in range(1, parts_ref.shape[0]):
        total += parts_ref[part].astype(F32)
    stream = tokens_ref[...] + mod_ref[2:3, :] * total
    stream_ref[...] = stream
    centred, table = centre(stream)
    sent_ref[:, : stream.shape[1]] = centred
    sent_ref[:, stream.shape[1] :] = table.astype(BF16)


def join(where, parts, tokens, mod):
    count, rows, width = parts.shape
    tile = BLOCK
    return pl.pallas_call(
        join_kernel,
        grid_spec=pltpu.PrefetchScalarGridSpec(
            num_scalar_prefetch=1,
            grid=(rows // tile,),
            in_specs=[
                pl.BlockSpec((count, tile, width), lambda i, w: (0, i, 0)),
                pl.BlockSpec((tile, width), lambda i, w: (i, 0)),
                pl.BlockSpec((3, width), lambda i, w: (0, w[2])),
            ],
            out_specs=[
                pl.BlockSpec((tile, width), lambda i, w: (i, 0)),
                pl.BlockSpec((tile, width + 128), lambda i, w: (i, 0)),
            ],
        ),
        out_shape=[
            jax.ShapeDtypeStruct((rows, width), F32),
            jax.ShapeDtypeStruct((rows, width + 128), BF16),
        ],
        compiler_params=params(),
        name="join",
    )(where, parts, tokens, mod)


def total_kernel(parts_ref, out_ref):
    total = parts_ref[0].astype(F32)
    for part in range(1, parts_ref.shape[0]):
        total += parts_ref[part].astype(F32)
    out_ref[...] = total.astype(BF16)


def total_of(parts):
    count, rows, width = parts.shape
    tile = BLOCK
    return pl.pallas_call(
        total_kernel,
        grid=(rows // tile,),
        in_specs=[pl.BlockSpec((count, tile, width), lambda i: (0, i, 0))],
        out_specs=pl.BlockSpec((tile, width), lambda i: (i, 0)),
        out_shape=jax.ShapeDtypeStruct((rows, width), BF16),
        compiler_params=params(),
        name="total_of",
    )(parts)


def time_kernel(frames, parts_ref, stats_ref, weight_ref, offset_ref, shift_ref, out_weight_ref, out_ref,
                att_ref, acc_ref, table_ref):
    accumulate_qkv(parts_ref, stats_ref, weight_ref, offset_ref, shift_ref, acc_ref, table_ref)

    @pl.when(pl.program_id(0) == pl.num_programs(0) - 1)
    def _():
        rows, packed_width = acc_ref.shape
        heads_width = packed_width // 3
        places = rows // frames
        group = 8
        span = frames * group
        row_place = lax.broadcasted_iota(jnp.int32, (span, span), 0) % group
        col_place = lax.broadcasted_iota(jnp.int32, (span, span), 1) % group
        bias = jnp.where(row_place == col_place, 0.0, -jnp.inf).astype(F32)
        packed = acc_ref[...].reshape(frames, places, packed_width)
        for start in range(0, places, group):
            chunk = packed[:, start : start + group, :].reshape(span, packed_width).astype(BF16)
            for head in range(heads_width // HD):
                low = head * HD
                query = chunk[:, low : low + HD]
                key = chunk[:, heads_width + low : heads_width + low + HD]
                value = chunk[:, 2 * heads_width + low : 2 * heads_width + low + HD]
                scores = lax.dot_general(
                    query, key, (((1,), (1,)), ((), ())), preferred_element_type=F32
                ) * SCALE + bias
                lifted = jnp.exp(scores - jnp.max(scores, axis=1, keepdims=True))
                norm = jnp.sum(lifted, axis=1, keepdims=True)
                mixed = jnp.dot(lifted.astype(BF16), value, preferred_element_type=F32) / norm
                att_ref[:, start : start + group, low : low + HD] = mixed.reshape(frames, group, HD)
        attended = att_ref[...].reshape(rows, heads_width).astype(BF16)
        project_out(attended, out_weight_ref, out_ref)


def time_layer(parts, folded, out_weight, rows, frames):
    count, _, width = parts.shape
    heads_width = folded[0].shape[2]
    grid, in_specs, scratch, cost = qkv_specs(parts, rows, heads_width)
    return pl.pallas_call(
        functools.partial(time_kernel, frames),
        grid=grid,
        in_specs=in_specs + [whole(out_weight.shape)],
        out_specs=whole((count, rows, width)),
        out_shape=jax.ShapeDtypeStruct((count, rows, width), BF16),
        scratch_shapes=[pltpu.VMEM((frames, rows // frames, heads_width), F32)] + scratch,
        compiler_params=params(),
        cost_estimate=cost,
        name="time_layer",
    )(parts, parts, *folded, out_weight)


def on_device(tokens, block_mask, space_qkv, space_out, space_mod, time_qkv, time_out, time_mod):
    videos, rows, width = tokens.shape
    parts = lax.axis_size("fsdp")
    seq_count = lax.axis_size("seq")
    frames = seq_count // 2
    seq_index = lax.axis_index("seq")
    where = jnp.stack([seq_index // 2, seq_index % 2, lax.axis_index("fsdp")]).astype(jnp.int32)
    same_half = [[2 * frame + half for frame in range(frames)] for half in range(2)]

    def across_frames(values):
        return lax.all_to_all(
            values.reshape(frames, rows // frames, -1), "seq", split_axis=0, concat_axis=0,
            tiled=True, axis_index_groups=same_half,
        ).reshape(rows, -1)

    def across_parts(values):
        return lax.all_to_all(values, "fsdp", split_axis=0, concat_axis=0, tiled=True)

    local = tokens.reshape(rows, width)
    space_folded = fold(space_mod, jnp.swapaxes(space_qkv, 0, 1), parts)
    time_folded = fold(time_mod, jnp.swapaxes(time_qkv, 0, 1), parts)
    queries, own = space_in(across_parts(pack(local, parts)), space_folded, rows)
    other = lax.ppermute(own, "seq", [(i, i ^ 1) for i in range(seq_count)])
    partial = space_attend(where, block_mask.reshape(-1), queries, own, other, space_out, parts)
    stream, sent = join(where, across_parts(partial), local, space_mod)
    wide = across_parts(repack(across_frames(sent), parts))
    partial_time = time_layer(wide, time_folded, time_out, rows, frames)
    returned = across_frames(total_of(across_parts(partial_time)))
    gate = lax.dynamic_slice_in_dim(time_mod[2], lax.axis_index("fsdp") * width, width, 0)
    return (stream + gate * returned.astype(F32)).reshape(tokens.shape)


def solution(mesh):
    placed = (
        P(None, "seq", "fsdp"),
        P(),
        P(None, None, "fsdp"),
        P("fsdp", None),
        P(),
        P(None, None, "fsdp"),
        P("fsdp", None),
        P(),
    )
    return jax.shard_map(
        on_device, mesh=mesh, in_specs=placed, out_specs=P(None, "seq", "fsdp"), check_vma=False
    )
```

```python
import functools
import math

import jax
import jax.numpy as jnp
from jax import lax
from jax.experimental import pallas as pl
from jax.experimental.pallas import tpu as pltpu
from jax.sharding import PartitionSpec as P

HD = 128
BLOCK = 128
EPS = 1e-06
SCALE = 1.0 / math.sqrt(HD)
VMEM_LIMIT = 48 * 1024 * 1024
F32 = jnp.float32
BF16 = jnp.bfloat16
STAT_ROWS = 8


def whole(shape):
    return pl.BlockSpec(shape, lambda *_: (0,) * len(shape))


def params():
    return pltpu.CompilerParams(vmem_limit_bytes=VMEM_LIMIT)


def spread_columns(columns, rows):
    lane = lax.broadcasted_iota(jnp.int32, (rows, 128), 1)
    table = jnp.zeros((rows, 128), F32)
    for index, column in enumerate(columns):
        table = jnp.where(lane == index, column, table)
    return table


def bf16_terms(values, count):
    terms = []
    for _ in range(count):
        term = values.astype(BF16).astype(F32)
        terms.append(term)
        values = values - term
    return terms


def centre(values):
    mean = jnp.sum(values, axis=1, keepdims=True) / values.shape[1]
    centred = values - mean
    squares = jnp.sum(centred * centred, axis=1, keepdims=True)
    table = spread_columns(bf16_terms(mean, 3) + bf16_terms(squares, 2), values.shape[0])
    return centred.astype(BF16), table


def pack_kernel(tokens_ref, out_ref):
    rows = tokens_ref.shape[0]
    centred, table = centre(tokens_ref[...])
    out_ref[:rows, :] = centred
    out_ref[rows:, :] = jnp.transpose(table)[:STAT_ROWS].astype(BF16)


def pack(tokens):
    rows, width = tokens.shape
    shape = (rows + STAT_ROWS, width)
    return pl.pallas_call(
        pack_kernel,
        grid=(1,),
        in_specs=[whole(tokens.shape)],
        out_specs=whole(shape),
        out_shape=jax.ShapeDtypeStruct(shape, BF16),
        compiler_params=params(),
        name="pack",
    )(tokens)


def repack_kernel(arrived_ref, out_ref):
    rows = arrived_ref.shape[0]
    width = out_ref.shape[1]
    out_ref[:rows, :] = arrived_ref[:, :width]
    out_ref[rows:, :] = jnp.transpose(arrived_ref[:, width:].astype(F32))[:STAT_ROWS].astype(BF16)


def repack(arrived):
    rows, width = arrived.shape
    shape = (rows + STAT_ROWS, width - 128)
    return pl.pallas_call(
        repack_kernel,
        grid=(1,),
        in_specs=[whole(arrived.shape)],
        out_specs=whole(shape),
        out_shape=jax.ShapeDtypeStruct(shape, BF16),
        compiler_params=params(),
        name="repack",
    )(arrived)


def row_table(stats_ref, width):
    parts, _, rows = stats_ref.shape
    line = lax.broadcasted_iota(jnp.int32, (parts, rows), 0)
    means = jnp.zeros((parts, rows), F32)
    squares = 0.0
    for part in range(parts):
        lines = stats_ref[part].astype(F32)
        means = jnp.where(line == part, lines[0:1] + lines[1:2] + lines[2:3], means)
        squares = squares + (lines[3:4] + lines[4:5])
    offsets = means - jnp.sum(means, axis=0, keepdims=True) / parts
    between = jnp.sum(offsets * offsets, axis=0, keepdims=True) * width
    scale = lax.rsqrt((squares + between) / (parts * width) + EPS)
    scales = jnp.broadcast_to(scale, (128 - parts, rows))
    return jnp.transpose(jnp.concatenate([offsets, scales], axis=0))


def modulate(parts_ref, mod_ref, normed_ref):
    parts, total_rows, width = parts_ref.shape
    rows = normed_ref.shape[0]
    table = row_table(parts_ref.at[:, rows:total_rows, :], width)
    scale = jnp.broadcast_to(table[:, 127:128], (rows, 128))
    for part in range(parts):
        offset = jnp.broadcast_to(table[:, part : part + 1], (rows, 128))
        for start in range(0, width, 128):
            columns = slice(part * width + start, part * width + start + 128)
            values = parts_ref[part, :rows, start : start + 128].astype(F32)
            gain = 1.0 + mod_ref[1:2, columns]
            normed_ref[:, columns] = (
                ((values + offset) * scale) * gain + mod_ref[0:1, columns]
            ).astype(BF16)


def qkv_specs(parts, mod, weight):
    count, _, width = parts.shape
    model_width, heads_width = weight.shape[1:]
    in_specs = [
        whole(parts.shape),
        whole(mod.shape),
        pl.BlockSpec((1, model_width, heads_width), lambda k: (k, 0, 0)),
    ]
    return in_specs


def space_in_kernel(parts_ref, mod_ref, weight_ref, q_ref, kv_ref, normed_ref):
    step = pl.program_id(0)

    @pl.when(step == 0)
    def _():
        modulate(parts_ref, mod_ref, normed_ref)

    product = jnp.dot(normed_ref[...], weight_ref[0], preferred_element_type=F32).astype(BF16)

    @pl.when(step == 0)
    def _():
        q_ref[0] = product

    @pl.when(step > 0)
    def _():
        kv_ref[step - 1] = product


def space_in(parts, mod, weight, rows):
    model_width, heads_width = weight.shape[1:]
    return pl.pallas_call(
        space_in_kernel,
        grid=(3,),
        in_specs=qkv_specs(parts, mod, weight),
        out_specs=[whole((1, rows, heads_width)), whole((2, rows, heads_width))],
        out_shape=[
            jax.ShapeDtypeStruct((1, rows, heads_width), BF16),
            jax.ShapeDtypeStruct((2, rows, heads_width), BF16),
        ],
        scratch_shapes=[pltpu.VMEM((rows, model_width), BF16)],
        compiler_params=params(),
        cost_estimate=pl.CostEstimate(
            flops=2 * rows * weight.size,
            bytes_accessed=2 * (weight.size + parts.size),
            transcendentals=0,
        ),
        name="space_in",
    )(parts, mod, weight)


def project_out(attended, weight_ref, out_ref):
    blocks, _, width = out_ref.shape
    for block in range(blocks):
        out_ref[block] = jnp.dot(
            attended, weight_ref[:, block * width : (block + 1) * width], preferred_element_type=F32
        ).astype(BF16)


def space_attend_kernel(where_ref, mask_ref, q_ref, own_ref, other_ref, weight_ref, out_ref):
    _, rows, heads_width = q_ref.shape
    query_blocks = rows // BLOCK
    key_blocks = 2 * query_blocks
    frame, half = where_ref[0], where_ref[1]
    mask_base = (frame * key_blocks + half * query_blocks) * key_blocks
    heads = []
    for head in range(heads_width // HD):
        key_cols = slice(head * HD, (head + 1) * HD)
        keys = [own_ref[0, :, key_cols], other_ref[0, :, key_cols]]
        values = [own_ref[1, :, key_cols], other_ref[1, :, key_cols]]
        pieces = []
        for block in range(query_blocks):
            query = q_ref[0, block * BLOCK : (block + 1) * BLOCK, key_cols]
            scored = []
            for side in range(2):
                scores = lax.dot_general(
                    query, keys[side], (((1,), (1,)), ((), ())), preferred_element_type=F32
                )
                side_half = half if side == 0 else 1 - half
                for key_block in range(query_blocks):
                    kept = mask_ref[
                        mask_base + block * key_blocks + side_half * query_blocks + key_block
                    ]
                    bias = jnp.where(kept == 1, 0.0, -jnp.inf).astype(F32)
                    scored.append(
                        scores[:, key_block * BLOCK : (key_block + 1) * BLOCK] * SCALE + bias
                    )
            scored = jnp.concatenate(scored, axis=1)
            row_max = jnp.max(scored, axis=1, keepdims=True)
            lifted = jnp.exp(scored - row_max)
            norm = jnp.sum(lifted, axis=1, keepdims=True)
            lifted = lifted.astype(BF16)
            mixed = jnp.dot(lifted[:, :rows], values[0], preferred_element_type=F32)
            mixed += jnp.dot(lifted[:, rows:], values[1], preferred_element_type=F32)
            pieces.append((mixed / norm).astype(BF16))
        heads.append(jnp.concatenate(pieces, axis=0))
    project_out(jnp.concatenate(heads, axis=1), weight_ref, out_ref)


def space_attend(where, mask, queries, own, other, weight, blocks):
    _, rows, heads_width = queries.shape
    width = weight.shape[1] // blocks
    return pl.pallas_call(
        space_attend_kernel,
        grid_spec=pltpu.PrefetchScalarGridSpec(
            num_scalar_prefetch=2,
            grid=(1,),
            in_specs=[
                whole(queries.shape),
                whole(own.shape),
                whole(other.shape),
                whole(weight.shape),
            ],
            out_specs=whole((blocks, rows, width)),
        ),
        out_shape=jax.ShapeDtypeStruct((blocks, rows, width), BF16),
        compiler_params=params(),
        cost_estimate=pl.CostEstimate(
            flops=2 * rows * heads_width * (4 * rows + weight.shape[1]),
            bytes_accessed=2 * (weight.size + rows * weight.shape[1] + 5 * rows * heads_width),
            transcendentals=2 * rows * rows * heads_width // HD,
        ),
        name="space_attend",
    )(where, mask, queries, own, other, weight)


def join_kernel(where_ref, parts_ref, tokens_ref, mod_ref, stream_ref, sent_ref):
    total = parts_ref[0].astype(F32)
    for part in range(1, parts_ref.shape[0]):
        total += parts_ref[part].astype(F32)
    stream = tokens_ref[...] + mod_ref[2:3, :] * total
    stream_ref[...] = stream
    centred, table = centre(stream)
    sent_ref[:, : stream.shape[1]] = centred
    sent_ref[:, stream.shape[1] :] = table.astype(BF16)


def join(where, parts, tokens, mod):
    count, rows, width = parts.shape
    tile = BLOCK
    return pl.pallas_call(
        join_kernel,
        grid_spec=pltpu.PrefetchScalarGridSpec(
            num_scalar_prefetch=1,
            grid=(rows // tile,),
            in_specs=[
                pl.BlockSpec((count, tile, width), lambda i, w: (0, i, 0)),
                pl.BlockSpec((tile, width), lambda i, w: (i, 0)),
                pl.BlockSpec((3, width), lambda i, w: (0, w[2])),
            ],
            out_specs=[
                pl.BlockSpec((tile, width), lambda i, w: (i, 0)),
                pl.BlockSpec((tile, width + 128), lambda i, w: (i, 0)),
            ],
        ),
        out_shape=[
            jax.ShapeDtypeStruct((rows, width), F32),
            jax.ShapeDtypeStruct((rows, width + 128), BF16),
        ],
        compiler_params=params(),
        name="join",
    )(where, parts, tokens, mod)


def total_kernel(parts_ref, out_ref):
    total = parts_ref[0].astype(F32)
    for part in range(1, parts_ref.shape[0]):
        total += parts_ref[part].astype(F32)
    out_ref[...] = total.astype(BF16)


def total_of(parts):
    count, rows, width = parts.shape
    tile = BLOCK
    return pl.pallas_call(
        total_kernel,
        grid=(rows // tile,),
        in_specs=[pl.BlockSpec((count, tile, width), lambda i: (0, i, 0))],
        out_specs=pl.BlockSpec((tile, width), lambda i: (i, 0)),
        out_shape=jax.ShapeDtypeStruct((rows, width), BF16),
        compiler_params=params(),
        name="total_of",
    )(parts)


def time_kernel(frames, parts_ref, mod_ref, weight_ref, out_weight_ref, out_ref,
                normed_ref, packed_ref, att_ref):
    step, last = pl.program_id(0), pl.num_programs(0) - 1

    @pl.when(step == 0)
    def _():
        modulate(parts_ref, mod_ref, normed_ref)

    packed_ref[step] = jnp.dot(
        normed_ref[...], weight_ref[0], preferred_element_type=F32
    ).reshape(packed_ref.shape[1:])

    @pl.when(step == last)
    def _():
        _, _, places, heads_width = packed_ref.shape
        group = 8
        span = frames * group
        row_place = lax.broadcasted_iota(jnp.int32, (span, span), 0) % group
        col_place = lax.broadcasted_iota(jnp.int32, (span, span), 1) % group
        bias = jnp.where(row_place == col_place, 0.0, -jnp.inf).astype(F32)
        for start in range(0, places, group):
            for low in range(0, heads_width, HD):
                query, key, value = [
                    packed_ref[part, :, start : start + group, low : low + HD]
                    .reshape(span, HD)
                    .astype(BF16)
                    for part in range(3)
                ]
                scores = lax.dot_general(
                    query, key, (((1,), (1,)), ((), ())), preferred_element_type=F32
                ) * SCALE + bias
                lifted = jnp.exp(scores - jnp.max(scores, axis=1, keepdims=True))
                norm = jnp.sum(lifted, axis=1, keepdims=True)
                mixed = jnp.dot(lifted.astype(BF16), value, preferred_element_type=F32) / norm
                att_ref[:, start : start + group, low : low + HD] = mixed.reshape(frames, group, HD)
        attended = att_ref[...].reshape(frames * places, heads_width).astype(BF16)
        project_out(attended, out_weight_ref, out_ref)


def time_layer(parts, mod, weight, out_weight, rows, frames):
    count, _, width = parts.shape
    model_width, heads_width = weight.shape[1:]
    return pl.pallas_call(
        functools.partial(time_kernel, frames),
        grid=(3,),
        in_specs=qkv_specs(parts, mod, weight) + [whole(out_weight.shape)],
        out_specs=whole((count, rows, width)),
        out_shape=jax.ShapeDtypeStruct((count, rows, width), BF16),
        scratch_shapes=[
            pltpu.VMEM((rows, model_width), BF16),
            pltpu.VMEM((3, frames, rows // frames, heads_width), F32),
            pltpu.VMEM((frames, rows // frames, heads_width), F32),
        ],
        compiler_params=params(),
        cost_estimate=pl.CostEstimate(
            flops=2 * rows * (weight.size + out_weight.size),
            bytes_accessed=2 * (weight.size + out_weight.size + 2 * parts.size),
            transcendentals=rows * BLOCK * heads_width // HD,
        ),
        name="time_layer",
    )(parts, mod, weight, out_weight)


def on_device(tokens, block_mask, space_qkv, space_out, space_mod, time_qkv, time_out, time_mod):
    videos, rows, width = tokens.shape
    parts = lax.axis_size("fsdp")
    seq_count = lax.axis_size("seq")
    frames = seq_count // 2
    seq_index = lax.axis_index("seq")
    where = jnp.stack([seq_index // 2, seq_index % 2, lax.axis_index("fsdp")]).astype(jnp.int32)
    same_half = [[2 * frame + half for frame in range(frames)] for half in range(2)]

    def across_frames(values):
        return lax.all_to_all(
            values.reshape(frames, rows // frames, -1), "seq", split_axis=0, concat_axis=0,
            tiled=True, axis_index_groups=same_half,
        ).reshape(rows, -1)

    def across_parts(values):
        return lax.all_to_all(values, "fsdp", split_axis=0, concat_axis=0, tiled=True)

    def gathered(shard):
        return across_parts(jnp.broadcast_to(shard[None], (parts,) + shard.shape))

    local = tokens.reshape(rows, width)
    queries, own = space_in(gathered(pack(local)), space_mod, jnp.swapaxes(space_qkv, 0, 1), rows)
    other = lax.ppermute(own, "seq", [(i, i ^ 1) for i in range(seq_count)])
    partial = space_attend(where, block_mask.reshape(-1), queries, own, other, space_out, parts)
    stream, sent = join(where, across_parts(partial), local, space_mod)
    wide = gathered(repack(across_frames(sent)))
    partial_time = time_layer(wide, time_mod, jnp.swapaxes(time_qkv, 0, 1), time_out, rows, frames)
    returned = across_frames(total_of(across_parts(partial_time)))
    gate = lax.dynamic_slice_in_dim(time_mod[2], lax.axis_index("fsdp") * width, width, 0)
    return (stream + gate * returned.astype(F32)).reshape(tokens.shape)


def solution(mesh):
    placed = (
        P(None, "seq", "fsdp"),
        P(),
        P(None, None, "fsdp"),
        P("fsdp", None),
        P(),
        P(None, None, "fsdp"),
        P("fsdp", None),
        P(),
    )
    return jax.shard_map(
        on_device, mesh=mesh, in_specs=placed, out_specs=P(None, "seq", "fsdp"), check_vma=False
    )
```

```python
import functools
import math

import jax
import jax.numpy as jnp
from jax import lax
from jax.experimental import pallas as pl
from jax.experimental.pallas import tpu as pltpu
from jax.sharding import PartitionSpec as P

HD = 128
BLOCK = 128
EPS = 1e-06
SCALE = 1.0 / math.sqrt(HD)
VMEM_LIMIT = 48 * 1024 * 1024
F32 = jnp.float32
BF16 = jnp.bfloat16
STAT_ROWS = 8


def whole(shape):
    return pl.BlockSpec(shape, lambda *_: (0,) * len(shape))


def params():
    return pltpu.CompilerParams(vmem_limit_bytes=VMEM_LIMIT)


def spread_columns(columns, rows):
    lane = lax.broadcasted_iota(jnp.int32, (rows, 128), 1)
    table = jnp.zeros((rows, 128), F32)
    for index, column in enumerate(columns):
        table = jnp.where(lane == index, column, table)
    return table


def bf16_terms(values, count):
    terms = []
    for _ in range(count):
        term = values.astype(BF16).astype(F32)
        terms.append(term)
        values = values - term
    return terms


def centre(values):
    mean = jnp.sum(values, axis=1, keepdims=True) / values.shape[1]
    centred = values - mean
    squares = jnp.sum(centred * centred, axis=1, keepdims=True)
    table = spread_columns(bf16_terms(mean, 3) + bf16_terms(squares, 2), values.shape[0])
    return centred.astype(BF16), table


def pack_kernel(tokens_ref, out_ref):
    rows = tokens_ref.shape[0]
    centred, table = centre(tokens_ref[...].astype(F32))
    out_ref[:rows, :] = centred
    out_ref[rows:, :] = jnp.transpose(table)[:STAT_ROWS].astype(BF16)


def pack(tokens):
    rows, width = tokens.shape
    shape = (rows + STAT_ROWS, width)
    return pl.pallas_call(
        pack_kernel,
        grid=(1,),
        in_specs=[whole(tokens.shape)],
        out_specs=whole(shape),
        out_shape=jax.ShapeDtypeStruct(shape, BF16),
        compiler_params=params(),
        name="pack",
    )(tokens)


def row_table(stats_ref, width):
    parts, _, rows = stats_ref.shape
    line = lax.broadcasted_iota(jnp.int32, (parts, rows), 0)
    means = jnp.zeros((parts, rows), F32)
    squares = 0.0
    for part in range(parts):
        lines = stats_ref[part].astype(F32)
        means = jnp.where(line == part, lines[0:1] + lines[1:2] + lines[2:3], means)
        squares = squares + (lines[3:4] + lines[4:5])
    offsets = means - jnp.sum(means, axis=0, keepdims=True) / parts
    between = jnp.sum(offsets * offsets, axis=0, keepdims=True) * width
    scale = lax.rsqrt((squares + between) / (parts * width) + EPS)
    scales = jnp.broadcast_to(scale, (128 - parts, rows))
    return jnp.transpose(jnp.concatenate([offsets, scales], axis=0))


def modulate(parts_ref, mod_ref, normed_ref):
    parts, total_rows, width = parts_ref.shape
    rows = normed_ref.shape[0]
    table = row_table(parts_ref.at[:, rows:total_rows, :], width)
    scale = jnp.broadcast_to(table[:, 127:128], (rows, 128))
    for part in range(parts):
        offset = jnp.broadcast_to(table[:, part : part + 1], (rows, 128))
        for start in range(0, width, 128):
            columns = slice(part * width + start, part * width + start + 128)
            values = parts_ref[part, :rows, start : start + 128].astype(F32)
            gain = 1.0 + mod_ref[1:2, columns]
            normed_ref[:, columns] = (
                ((values + offset) * scale) * gain + mod_ref[0:1, columns]
            ).astype(BF16)


def qkv_specs(parts, mod, weight):
    count, _, width = parts.shape
    model_width, heads_width = weight.shape[1:]
    in_specs = [
        whole(parts.shape),
        whole(mod.shape),
        pl.BlockSpec((1, model_width, heads_width), lambda k: (k, 0, 0)),
    ]
    return in_specs


def space_in_kernel(parts_ref, mod_ref, weight_ref, q_ref, kv_ref, normed_ref):
    step = pl.program_id(0)

    @pl.when(step == 0)
    def _():
        modulate(parts_ref, mod_ref, normed_ref)

    product = jnp.dot(normed_ref[...], weight_ref[0], preferred_element_type=F32).astype(BF16)

    @pl.when(step == 0)
    def _():
        q_ref[0] = product

    @pl.when(step > 0)
    def _():
        kv_ref[step - 1] = product


def space_in(parts, mod, weight, rows):
    model_width, heads_width = weight.shape[1:]
    return pl.pallas_call(
        space_in_kernel,
        grid=(3,),
        in_specs=qkv_specs(parts, mod, weight),
        out_specs=[whole((1, rows, heads_width)), whole((2, rows, heads_width))],
        out_shape=[
            jax.ShapeDtypeStruct((1, rows, heads_width), BF16),
            jax.ShapeDtypeStruct((2, rows, heads_width), BF16),
        ],
        scratch_shapes=[pltpu.VMEM((rows, model_width), BF16)],
        compiler_params=params(),
        cost_estimate=pl.CostEstimate(
            flops=2 * rows * weight.size,
            bytes_accessed=2 * (weight.size + parts.size),
            transcendentals=0,
        ),
        name="space_in",
    )(parts, mod, weight)


def project_out(attended, weight_ref, out_ref):
    blocks, _, width = out_ref.shape
    for block in range(blocks):
        out_ref[block] = jnp.dot(
            attended, weight_ref[:, block * width : (block + 1) * width], preferred_element_type=F32
        ).astype(BF16)


def space_attend_kernel(where_ref, mask_ref, q_ref, own_ref, other_ref, weight_ref, out_ref):
    _, rows, heads_width = q_ref.shape
    query_blocks = rows // BLOCK
    key_blocks = 2 * query_blocks
    frame, half = where_ref[0], where_ref[1]
    mask_base = (frame * key_blocks + half * query_blocks) * key_blocks
    heads = []
    for head in range(heads_width // HD):
        key_cols = slice(head * HD, (head + 1) * HD)
        keys = [own_ref[0, :, key_cols], other_ref[0, :, key_cols]]
        values = [own_ref[1, :, key_cols], other_ref[1, :, key_cols]]
        pieces = []
        for block in range(query_blocks):
            query = q_ref[0, block * BLOCK : (block + 1) * BLOCK, key_cols]
            scored = []
            for side in range(2):
                scores = lax.dot_general(
                    query, keys[side], (((1,), (1,)), ((), ())), preferred_element_type=F32
                )
                side_half = half if side == 0 else 1 - half
                for key_block in range(query_blocks):
                    kept = mask_ref[
                        mask_base + block * key_blocks + side_half * query_blocks + key_block
                    ]
                    bias = jnp.where(kept == 1, 0.0, -jnp.inf).astype(F32)
                    scored.append(
                        scores[:, key_block * BLOCK : (key_block + 1) * BLOCK] * SCALE + bias
                    )
            scored = jnp.concatenate(scored, axis=1)
            row_max = jnp.max(scored, axis=1, keepdims=True)
            lifted = jnp.exp(scored - row_max)
            norm = jnp.sum(lifted, axis=1, keepdims=True)
            lifted = lifted.astype(BF16)
            mixed = jnp.dot(lifted[:, :rows], values[0], preferred_element_type=F32)
            mixed += jnp.dot(lifted[:, rows:], values[1], preferred_element_type=F32)
            pieces.append((mixed / norm).astype(BF16))
        heads.append(jnp.concatenate(pieces, axis=0))
    project_out(jnp.concatenate(heads, axis=1), weight_ref, out_ref)


def space_attend(where, mask, queries, own, other, weight, blocks):
    _, rows, heads_width = queries.shape
    width = weight.shape[1] // blocks
    return pl.pallas_call(
        space_attend_kernel,
        grid_spec=pltpu.PrefetchScalarGridSpec(
            num_scalar_prefetch=2,
            grid=(1,),
            in_specs=[
                whole(queries.shape),
                whole(own.shape),
                whole(other.shape),
                whole(weight.shape),
            ],
            out_specs=whole((blocks, rows, width)),
        ),
        out_shape=jax.ShapeDtypeStruct((blocks, rows, width), BF16),
        compiler_params=params(),
        cost_estimate=pl.CostEstimate(
            flops=2 * rows * heads_width * (4 * rows + weight.shape[1]),
            bytes_accessed=2 * (weight.size + rows * weight.shape[1] + 5 * rows * heads_width),
            transcendentals=2 * rows * rows * heads_width // HD,
        ),
        name="space_attend",
    )(where, mask, queries, own, other, weight)


def join_kernel(where_ref, parts_ref, tokens_ref, mod_ref, stream_ref, sent_ref):
    total = parts_ref[0].astype(F32)
    for part in range(1, parts_ref.shape[0]):
        total += parts_ref[part].astype(F32)
    stream = tokens_ref[...] + mod_ref[2:3, :] * total
    stream_ref[...] = stream
    sent_ref[...] = stream.astype(BF16)


def join(where, parts, tokens, mod):
    count, rows, width = parts.shape
    tile = BLOCK
    return pl.pallas_call(
        join_kernel,
        grid_spec=pltpu.PrefetchScalarGridSpec(
            num_scalar_prefetch=1,
            grid=(rows // tile,),
            in_specs=[
                pl.BlockSpec((count, tile, width), lambda i, w: (0, i, 0)),
                pl.BlockSpec((tile, width), lambda i, w: (i, 0)),
                pl.BlockSpec((3, width), lambda i, w: (0, w[2])),
            ],
            out_specs=[
                pl.BlockSpec((tile, width), lambda i, w: (i, 0)),
                pl.BlockSpec((tile, width), lambda i, w: (i, 0)),
            ],
        ),
        out_shape=[
            jax.ShapeDtypeStruct((rows, width), F32),
            jax.ShapeDtypeStruct((rows, width), BF16),
        ],
        compiler_params=params(),
        name="join",
    )(where, parts, tokens, mod)


def time_kernel(frames, parts_ref, mod_ref, weight_ref, out_weight_ref, out_ref,
                normed_ref, packed_ref, att_ref):
    step, last = pl.program_id(0), pl.num_programs(0) - 1

    @pl.when(step == 0)
    def _():
        modulate(parts_ref, mod_ref, normed_ref)

    packed_ref[step] = jnp.dot(
        normed_ref[...], weight_ref[0], preferred_element_type=F32
    ).reshape(packed_ref.shape[1:])

    @pl.when(step == last)
    def _():
        _, _, places, heads_width = packed_ref.shape
        group = 8
        span = frames * group
        row_place = lax.broadcasted_iota(jnp.int32, (span, span), 0) % group
        col_place = lax.broadcasted_iota(jnp.int32, (span, span), 1) % group
        bias = jnp.where(row_place == col_place, 0.0, -jnp.inf).astype(F32)
        for start in range(0, places, group):
            for low in range(0, heads_width, HD):
                query, key, value = [
                    packed_ref[part, :, start : start + group, low : low + HD]
                    .reshape(span, HD)
                    .astype(BF16)
                    for part in range(3)
                ]
                scores = lax.dot_general(
                    query, key, (((1,), (1,)), ((), ())), preferred_element_type=F32
                ) * SCALE + bias
                lifted = jnp.exp(scores - jnp.max(scores, axis=1, keepdims=True))
                norm = jnp.sum(lifted, axis=1, keepdims=True)
                mixed = jnp.dot(lifted.astype(BF16), value, preferred_element_type=F32) / norm
                att_ref[:, start : start + group, low : low + HD] = mixed.reshape(frames, group, HD)
        attended = att_ref[...].reshape(frames * places, heads_width).astype(BF16)
        project_out(attended, out_weight_ref, out_ref)


def time_layer(parts, mod, weight, out_weight, rows, frames):
    count, _, width = parts.shape
    model_width, heads_width = weight.shape[1:]
    return pl.pallas_call(
        functools.partial(time_kernel, frames),
        grid=(3,),
        in_specs=qkv_specs(parts, mod, weight) + [whole(out_weight.shape)],
        out_specs=whole((count, rows, width)),
        out_shape=jax.ShapeDtypeStruct((count, rows, width), BF16),
        scratch_shapes=[
            pltpu.VMEM((rows, model_width), BF16),
            pltpu.VMEM((3, frames, rows // frames, heads_width), F32),
            pltpu.VMEM((frames, rows // frames, heads_width), F32),
        ],
        compiler_params=params(),
        cost_estimate=pl.CostEstimate(
            flops=2 * rows * (weight.size + out_weight.size),
            bytes_accessed=2 * (weight.size + out_weight.size + 2 * parts.size),
            transcendentals=rows * BLOCK * heads_width // HD,
        ),
        name="time_layer",
    )(parts, mod, weight, out_weight)


def on_device(tokens, block_mask, space_qkv, space_out, space_mod, time_qkv, time_out, time_mod):
    videos, rows, width = tokens.shape
    parts = lax.axis_size("fsdp")
    seq_count = lax.axis_size("seq")
    frames = seq_count // 2
    seq_index = lax.axis_index("seq")
    where = jnp.stack([seq_index // 2, seq_index % 2, lax.axis_index("fsdp")]).astype(jnp.int32)
    same_half = [[2 * frame + half for frame in range(frames)] for half in range(2)]

    def across_frames(values):
        return lax.all_to_all(
            values.reshape(frames, rows // frames, -1), "seq", split_axis=0, concat_axis=0,
            tiled=True, axis_index_groups=same_half,
        ).reshape(rows, -1)

    def across_parts(values):
        return lax.all_to_all(values, "fsdp", split_axis=0, concat_axis=0, tiled=True)

    def gathered(shard):
        return across_parts(jnp.broadcast_to(shard[None], (parts,) + shard.shape))

    local = tokens.reshape(rows, width)
    queries, own = space_in(gathered(pack(local)), space_mod, jnp.swapaxes(space_qkv, 0, 1), rows)
    other = lax.ppermute(own, "seq", [(i, i ^ 1) for i in range(seq_count)])
    partial = space_attend(where, block_mask.reshape(-1), queries, own, other, space_out, parts)
    stream, sent = join(where, across_parts(partial), local, space_mod)
    wide = gathered(pack(across_frames(sent)))
    partial_time = time_layer(wide, time_mod, jnp.swapaxes(time_qkv, 0, 1), time_out, rows, frames)
    total = jnp.sum(across_parts(partial_time).astype(F32), axis=0).astype(BF16)
    returned = across_frames(total)
    gate = lax.dynamic_slice_in_dim(time_mod[2], lax.axis_index("fsdp") * width, width, 0)
    return (stream + gate * returned.astype(F32)).reshape(tokens.shape)


def solution(mesh):
    placed = (
        P(None, "seq", "fsdp"),
        P(),
        P(None, None, "fsdp"),
        P("fsdp", None),
        P(),
        P(None, None, "fsdp"),
        P("fsdp", None),
        P(),
    )
    return jax.shard_map(
        on_device, mesh=mesh, in_specs=placed, out_specs=P(None, "seq", "fsdp"), check_vma=False
    )
```

```python
import functools
import math

import jax
import jax.numpy as jnp
from jax import lax
from jax.experimental import pallas as pl
from jax.experimental.pallas import tpu as pltpu
from jax.sharding import PartitionSpec as P

HD = 128
BLOCK = 128
EPS = 1e-06
SCALE = 1.0 / math.sqrt(HD)
VMEM_LIMIT = 24 * 1024 * 1024
ROW_TILE = 192
F32 = jnp.float32
BF16 = jnp.bfloat16
STAT_ROWS = 8


def vmem(count):
    return [pl.BlockSpec(memory_space=pltpu.VMEM)] * count


def smem(count):
    return [pl.BlockSpec(memory_space=pltpu.SMEM)] * count


def params():
    return pltpu.CompilerParams(vmem_limit_bytes=VMEM_LIMIT)


def spread_columns(columns, rows):
    lane = lax.broadcasted_iota(jnp.int32, (rows, 128), 1)
    table = jnp.zeros((rows, 128), F32)
    for index, column in enumerate(columns):
        table = jnp.where(lane == index, column, table)
    return table


def bf16_terms(values, count):
    terms = []
    for _ in range(count):
        term = values.astype(BF16).astype(F32)
        terms.append(term)
        values = values - term
    return terms


def centre(values):
    mean = jnp.sum(values, axis=1, keepdims=True) / values.shape[1]
    centred = values - mean
    squares = jnp.sum(centred * centred, axis=1, keepdims=True)
    table = spread_columns(bf16_terms(mean, 3) + bf16_terms(squares, 2), values.shape[0])
    return centred.astype(BF16), table


def pack_kernel(tokens_ref, out_ref):
    rows = tokens_ref.shape[0]
    centred, table = centre(tokens_ref[...].astype(F32))
    out_ref[:rows, :] = centred
    out_ref[rows:, :] = jnp.transpose(table)[:STAT_ROWS].astype(BF16)


def pack(tokens):
    rows, width = tokens.shape
    shape = (rows + STAT_ROWS, width)
    return pl.pallas_call(
        pack_kernel,
        in_specs=vmem(1),
        out_specs=vmem(1)[0],
        out_shape=jax.ShapeDtypeStruct(shape, BF16),
        compiler_params=params(),
        name="pack",
    )(tokens)


def row_table(stats_ref, width):
    parts, _, rows = stats_ref.shape
    line = lax.broadcasted_iota(jnp.int32, (parts, rows), 0)
    means = jnp.zeros((parts, rows), F32)
    squares = 0.0
    for part in range(parts):
        lines = stats_ref[part].astype(F32)
        means = jnp.where(line == part, lines[0:1] + lines[1:2] + lines[2:3], means)
        squares = squares + (lines[3:4] + lines[4:5])
    offsets = means - jnp.sum(means, axis=0, keepdims=True) / parts
    between = jnp.sum(offsets * offsets, axis=0, keepdims=True) * width
    scale = lax.rsqrt((squares + between) / (parts * width) + EPS)
    scales = jnp.broadcast_to(scale, (128 - parts, rows))
    return jnp.transpose(jnp.concatenate([offsets, scales], axis=0))


def modulate(parts_ref, mod_ref, normed_ref):
    parts, total_rows, width = parts_ref.shape
    rows = normed_ref.shape[0]
    table = row_table(parts_ref.at[:, rows:total_rows, :], width)
    scale = jnp.broadcast_to(table[:, 127:128], (rows, 128))
    for part in range(parts):
        offset = jnp.broadcast_to(table[:, part : part + 1], (rows, 128))
        for start in range(0, width, 128):
            columns = slice(part * width + start, part * width + start + 128)
            values = parts_ref[part, :rows, start : start + 128].astype(F32)
            gain = 1.0 + mod_ref[1:2, columns]
            normed_ref[:, columns] = (
                ((values + offset) * scale) * gain + mod_ref[0:1, columns]
            ).astype(BF16)


def qkv_rows(normed_ref, weight_ref):
    rows = normed_ref.shape[0]
    tile = ROW_TILE if rows % ROW_TILE == 0 else rows
    for which in range(3):
        for start in range(0, rows, tile):
            span = slice(start, start + tile)
            yield which, span, jnp.dot(
                normed_ref[span, :], weight_ref[which], preferred_element_type=F32
            )


def space_in_kernel(parts_ref, mod_ref, weight_ref, q_ref, kv_ref, normed_ref):
    modulate(parts_ref, mod_ref, normed_ref)
    for which, span, values in qkv_rows(normed_ref, weight_ref):
        if which == 0:
            q_ref[span, :] = values.astype(BF16)
        else:
            kv_ref[which - 1, span, :] = values.astype(BF16)


def space_in(parts, mod, weight, rows):
    model_width, heads_width = weight.shape[1:]
    return pl.pallas_call(
        space_in_kernel,
        in_specs=vmem(3),
        out_specs=vmem(2),
        out_shape=[
            jax.ShapeDtypeStruct((rows, heads_width), BF16),
            jax.ShapeDtypeStruct((2, rows, heads_width), BF16),
        ],
        scratch_shapes=[pltpu.VMEM((rows, model_width), BF16)],
        compiler_params=params(),
        cost_estimate=pl.CostEstimate(
            flops=2 * rows * weight.size,
            bytes_accessed=2 * (weight.size + parts.size),
            transcendentals=0,
        ),
        name="space_in",
    )(parts, mod, weight)


def project_out(attended, weight_ref, out_ref):
    blocks, _, width = out_ref.shape
    for block in range(blocks):
        out_ref[block] = jnp.dot(
            attended, weight_ref[:, block * width : (block + 1) * width], preferred_element_type=F32
        ).astype(BF16)


def soft(scores):
    lifted = [jnp.exp(entry - jnp.max(entry, axis=1, keepdims=True)) for entry in scores]
    norms = [jnp.sum(entry, axis=1, keepdims=True) for entry in lifted]
    return [entry.astype(BF16) for entry in lifted], norms


def against(query, keys):
    return lax.dot_general(query, keys, (((1,), (1,)), ((), ())), preferred_element_type=F32)


def space_attend_kernel(where_ref, mask_ref, q_ref, own_ref, other_ref, weight_ref, out_ref):
    rows, heads_width = q_ref.shape
    query_blocks = rows // BLOCK
    key_blocks = 2 * query_blocks
    half = where_ref[1]
    mask_base = (where_ref[0] * key_blocks + half * query_blocks) * key_blocks
    biases = []
    for block in range(query_blocks):
        line = []
        for side in range(2):
            first = (half if side == 0 else 1 - half) * query_blocks
            for key_block in range(query_blocks):
                kept = mask_ref[mask_base + block * key_blocks + first + key_block]
                line.append(jnp.where(kept == 1, 0.0, -jnp.inf).astype(F32))
        biases.append(line)
    heads = [slice(start, start + HD) for start in range(0, heads_width, HD)]
    keys = [jnp.concatenate([own_ref[0, :, head], other_ref[0, :, head]], axis=0) for head in heads]
    values = [jnp.concatenate([own_ref[1, :, head], other_ref[1, :, head]], axis=0) for head in heads]
    units = [(head, block) for head in range(len(heads)) for block in range(query_blocks)]
    scores = [
        against(q_ref[block * BLOCK : (block + 1) * BLOCK, heads[head]], keys[head])
        for head, block in units
    ]
    scores = [
        jnp.concatenate(
            [
                entry[:, index * BLOCK : (index + 1) * BLOCK] * SCALE + bias
                for index, bias in enumerate(biases[block])
            ],
            axis=1,
        )
        for (_, block), entry in zip(units, scores)
    ]
    lifted, norms = soft(scores)
    mixed = [
        (jnp.dot(entry, values[head], preferred_element_type=F32) / norm).astype(BF16)
        for (head, _), entry, norm in zip(units, lifted, norms)
    ]
    attended = [
        jnp.concatenate(mixed[head * query_blocks : (head + 1) * query_blocks], axis=0)
        for head in range(len(heads))
    ]
    project_out(jnp.concatenate(attended, axis=1), weight_ref, out_ref)


def space_attend(where, mask, queries, own, other, weight, blocks):
    rows, heads_width = queries.shape
    width = weight.shape[1] // blocks
    return pl.pallas_call(
        space_attend_kernel,
        in_specs=smem(2) + vmem(4),
        out_specs=vmem(1)[0],
        out_shape=jax.ShapeDtypeStruct((blocks, rows, width), BF16),
        compiler_params=params(),
        cost_estimate=pl.CostEstimate(
            flops=2 * rows * heads_width * (4 * rows + weight.shape[1]),
            bytes_accessed=2 * (weight.size + rows * weight.shape[1] + 5 * rows * heads_width),
            transcendentals=2 * rows * rows * heads_width // HD,
        ),
        name="space_attend",
    )(where, mask, queries, own, other, weight)


def local_gate(where_ref, mod_ref, width):
    return mod_ref[2:3, pl.ds(pl.multiple_of(where_ref[2] * width, 128), width)]


def join_kernel(where_ref, parts_ref, tokens_ref, mod_ref, stream_ref, sent_ref):
    total = parts_ref[0].astype(F32)
    for part in range(1, parts_ref.shape[0]):
        total += parts_ref[part].astype(F32)
    stream = tokens_ref[...] + local_gate(where_ref, mod_ref, total.shape[1]) * total
    stream_ref[...] = stream
    sent_ref[...] = stream.astype(BF16)


def join(where, parts, tokens, mod):
    count, rows, width = parts.shape
    return pl.pallas_call(
        join_kernel,
        in_specs=smem(1) + vmem(3),
        out_specs=vmem(2),
        out_shape=[
            jax.ShapeDtypeStruct((rows, width), F32),
            jax.ShapeDtypeStruct((rows, width), BF16),
        ],
        compiler_params=params(),
        name="join",
    )(where, parts, tokens, mod)


def time_kernel(parts_ref, mod_ref, weight_ref, out_weight_ref, out_ref, normed_ref, packed_ref, att_ref):
    modulate(parts_ref, mod_ref, normed_ref)
    frames, places, heads_width = att_ref.shape
    for which, span, values in qkv_rows(normed_ref, weight_ref):
        first = span.start // places
        count = values.shape[0] // places
        packed_ref[which, first : first + count] = values.reshape(count, places, heads_width)
    group = 8
    span = frames * group
    row_place = lax.broadcasted_iota(jnp.int32, (span, span), 0) % group
    col_place = lax.broadcasted_iota(jnp.int32, (span, span), 1) % group
    bias = jnp.where(row_place == col_place, 0.0, -jnp.inf).astype(F32)
    units = [(start, low) for start in range(0, places, group) for low in range(0, heads_width, HD)]

    def chosen(which, start, low):
        block = packed_ref[which, :, start : start + group, low : low + HD]
        return block.reshape(span, HD).astype(BF16)

    scores = [against(chosen(0, *unit), chosen(1, *unit)) * SCALE + bias for unit in units]
    lifted, norms = soft(scores)
    for unit, entry, norm in zip(units, lifted, norms):
        mixed = jnp.dot(entry, chosen(2, *unit), preferred_element_type=F32) / norm
        start, low = unit
        att_ref[:, start : start + group, low : low + HD] = mixed.reshape(frames, group, HD)
    project_out(att_ref[...].reshape(frames * places, heads_width).astype(BF16), out_weight_ref, out_ref)


def time_layer(parts, mod, weight, out_weight, rows, frames):
    count, _, width = parts.shape
    model_width, heads_width = weight.shape[1:]
    return pl.pallas_call(
        time_kernel,
        in_specs=vmem(4),
        out_specs=vmem(1)[0],
        out_shape=jax.ShapeDtypeStruct((count, rows, width), BF16),
        scratch_shapes=[
            pltpu.VMEM((rows, model_width), BF16),
            pltpu.VMEM((3, frames, rows // frames, heads_width), F32),
            pltpu.VMEM((frames, rows // frames, heads_width), F32),
        ],
        compiler_params=params(),
        cost_estimate=pl.CostEstimate(
            flops=2 * rows * (weight.size + out_weight.size),
            bytes_accessed=2 * (weight.size + out_weight.size + 2 * parts.size),
            transcendentals=rows * BLOCK * heads_width // HD,
        ),
        name="time_layer",
    )(parts, mod, weight, out_weight)


def on_device(tokens, block_mask, space_qkv, space_out, space_mod, time_qkv, time_out, time_mod):
    videos, rows, width = tokens.shape
    parts = lax.axis_size("fsdp")
    seq_count = lax.axis_size("seq")
    frames = seq_count // 2
    seq_index = lax.axis_index("seq")
    where = jnp.stack([seq_index // 2, seq_index % 2, lax.axis_index("fsdp")]).astype(jnp.int32)
    same_half = [[2 * frame + half for frame in range(frames)] for half in range(2)]

    def across_frames(values):
        return lax.all_to_all(
            values.reshape(frames, rows // frames, -1), "seq", split_axis=0, concat_axis=0,
            tiled=True, axis_index_groups=same_half,
        ).reshape(rows, -1)

    def across_parts(values):
        return lax.all_to_all(values, "fsdp", split_axis=0, concat_axis=0, tiled=True)

    def gathered(shard):
        return across_parts(jnp.broadcast_to(shard[None], (parts,) + shard.shape))

    local = tokens.reshape(rows, width)
    queries, own = space_in(gathered(pack(local)), space_mod, jnp.swapaxes(space_qkv, 0, 1), rows)
    other = lax.ppermute(own, "seq", [(i, i ^ 1) for i in range(seq_count)])
    partial = space_attend(where, block_mask.reshape(-1), queries, own, other, space_out, parts)
    stream, sent = join(where, across_parts(partial), local, space_mod)
    wide = gathered(pack(across_frames(sent)))
    partial_time = time_layer(wide, time_mod, jnp.swapaxes(time_qkv, 0, 1), time_out, rows, frames)
    total = jnp.sum(across_parts(partial_time).astype(F32), axis=0).astype(BF16)
    returned = across_frames(total)
    gate = lax.dynamic_slice_in_dim(time_mod[2], lax.axis_index("fsdp") * width, width, 0)
    return (stream + gate * returned.astype(F32)).reshape(tokens.shape)


def solution(mesh):
    placed = (
        P(None, "seq", "fsdp"),
        P(),
        P(None, None, "fsdp"),
        P("fsdp", None),
        P(),
        P(None, None, "fsdp"),
        P("fsdp", None),
        P(),
    )
    return jax.shard_map(
        on_device, mesh=mesh, in_specs=placed, out_specs=P(None, "seq", "fsdp"), check_vma=False
    )
```

```python
import functools
import math

import jax
import jax.numpy as jnp
from jax import lax
from jax.experimental import pallas as pl
from jax.experimental.pallas import tpu as pltpu
from jax.sharding import PartitionSpec as P

HD = 128
BLOCK = 128
EPS = 1e-06
SCALE = 1.0 / math.sqrt(HD)
VMEM_LIMIT = 24 * 1024 * 1024
ROW_TILE = 192
F32 = jnp.float32
BF16 = jnp.bfloat16
STAT_ROWS = 8


def vmem(count):
    return [pl.BlockSpec(memory_space=pltpu.VMEM)] * count


def smem(count):
    return [pl.BlockSpec(memory_space=pltpu.SMEM)] * count


def params():
    return pltpu.CompilerParams(vmem_limit_bytes=VMEM_LIMIT)


def spread_columns(columns, rows):
    lane = lax.broadcasted_iota(jnp.int32, (rows, 128), 1)
    table = jnp.zeros((rows, 128), F32)
    for index, column in enumerate(columns):
        table = jnp.where(lane == index, column, table)
    return table


def bf16_terms(values, count):
    terms = []
    for _ in range(count):
        term = values.astype(BF16).astype(F32)
        terms.append(term)
        values = values - term
    return terms


def centre(values):
    mean = jnp.sum(values, axis=1, keepdims=True) / values.shape[1]
    centred = values - mean
    squares = jnp.sum(centred * centred, axis=1, keepdims=True)
    table = spread_columns(bf16_terms(mean, 3) + bf16_terms(squares, 2), values.shape[0])
    return centred.astype(BF16), table


def pack_kernel(tokens_ref, out_ref):
    rows = tokens_ref.shape[0]
    centred, table = centre(tokens_ref[...].astype(F32))
    out_ref[:rows, :] = centred
    out_ref[rows:, :] = jnp.transpose(table)[:STAT_ROWS].astype(BF16)


def pack(tokens):
    rows, width = tokens.shape
    shape = (rows + STAT_ROWS, width)
    return pl.pallas_call(
        pack_kernel,
        in_specs=vmem(1),
        out_specs=vmem(1)[0],
        out_shape=jax.ShapeDtypeStruct(shape, BF16),
        compiler_params=params(),
        name="pack",
    )(tokens)


def row_table(stats_ref, width):
    parts, _, rows = stats_ref.shape
    line = lax.broadcasted_iota(jnp.int32, (parts, rows), 0)
    means = jnp.zeros((parts, rows), F32)
    squares = 0.0
    for part in range(parts):
        lines = stats_ref[part].astype(F32)
        means = jnp.where(line == part, lines[0:1] + lines[1:2] + lines[2:3], means)
        squares = squares + (lines[3:4] + lines[4:5])
    offsets = means - jnp.sum(means, axis=0, keepdims=True) / parts
    between = jnp.sum(offsets * offsets, axis=0, keepdims=True) * width
    scale = lax.rsqrt((squares + between) / (parts * width) + EPS)
    scales = jnp.broadcast_to(scale, (128 - parts, rows))
    return jnp.transpose(jnp.concatenate([offsets, scales], axis=0))


def modulate(parts_ref, mod_ref, normed_ref):
    parts, total_rows, width = parts_ref.shape
    rows = normed_ref.shape[0]
    table = row_table(parts_ref.at[:, rows:total_rows, :], width)
    scale = jnp.broadcast_to(table[:, 127:128], (rows, 128))
    for part in range(parts):
        offset = jnp.broadcast_to(table[:, part : part + 1], (rows, 128))
        for start in range(0, width, 128):
            columns = slice(part * width + start, part * width + start + 128)
            values = parts_ref[part, :rows, start : start + 128].astype(F32)
            gain = 1.0 + mod_ref[1:2, columns]
            normed_ref[:, columns] = (
                ((values + offset) * scale) * gain + mod_ref[0:1, columns]
            ).astype(BF16)


def qkv_rows(normed_ref, weight_ref):
    rows = normed_ref.shape[0]
    tile = ROW_TILE if rows % ROW_TILE == 0 else rows
    for which in range(3):
        for start in range(0, rows, tile):
            span = slice(start, start + tile)
            yield which, span, jnp.dot(
                normed_ref[span, :], weight_ref[which], preferred_element_type=F32
            )


def space_in_kernel(parts_ref, mod_ref, weight_ref, q_ref, kv_ref, normed_ref):
    modulate(parts_ref, mod_ref, normed_ref)
    for which, span, values in qkv_rows(normed_ref, weight_ref):
        if which == 0:
            q_ref[span, :] = values.astype(BF16)
        else:
            kv_ref[which - 1, span, :] = values.astype(BF16)


def space_in(parts, mod, weight, rows):
    model_width, heads_width = weight.shape[1:]
    return pl.pallas_call(
        space_in_kernel,
        in_specs=vmem(3),
        out_specs=vmem(2),
        out_shape=[
            jax.ShapeDtypeStruct((rows, heads_width), BF16),
            jax.ShapeDtypeStruct((2, rows, heads_width), BF16),
        ],
        scratch_shapes=[pltpu.VMEM((rows, model_width), BF16)],
        compiler_params=params(),
        cost_estimate=pl.CostEstimate(
            flops=2 * rows * weight.size,
            bytes_accessed=2 * (weight.size + parts.size),
            transcendentals=0,
        ),
        name="space_in",
    )(parts, mod, weight)


def soft(scores):
    lifted = [jnp.exp(entry - jnp.max(entry, axis=1, keepdims=True)) for entry in scores]
    norms = [jnp.sum(entry, axis=1, keepdims=True) for entry in lifted]
    return [entry.astype(BF16) for entry in lifted], norms


def against(query, keys):
    return lax.dot_general(query, keys, (((1,), (1,)), ((), ())), preferred_element_type=F32)


def space_attend_kernel(where_ref, mask_ref, q_ref, own_ref, other_ref, out_ref):
    rows, heads_width = q_ref.shape
    query_blocks = rows // BLOCK
    key_blocks = 2 * query_blocks
    half = where_ref[1]
    mask_base = (where_ref[0] * key_blocks + half * query_blocks) * key_blocks
    biases = []
    for block in range(query_blocks):
        line = []
        for side in range(2):
            first = (half if side == 0 else 1 - half) * query_blocks
            for key_block in range(query_blocks):
                kept = mask_ref[mask_base + block * key_blocks + first + key_block]
                line.append(jnp.where(kept == 1, 0.0, -jnp.inf).astype(F32))
        biases.append(line)
    heads = [slice(start, start + HD) for start in range(0, heads_width, HD)]
    keys = [jnp.concatenate([own_ref[0, :, head], other_ref[0, :, head]], axis=0) for head in heads]
    values = [jnp.concatenate([own_ref[1, :, head], other_ref[1, :, head]], axis=0) for head in heads]
    units = [(head, block) for head in range(len(heads)) for block in range(query_blocks)]
    scores = [
        against(q_ref[block * BLOCK : (block + 1) * BLOCK, heads[head]], keys[head])
        for head, block in units
    ]
    scores = [
        jnp.concatenate(
            [
                entry[:, index * BLOCK : (index + 1) * BLOCK] * SCALE + bias
                for index, bias in enumerate(biases[block])
            ],
            axis=1,
        )
        for (_, block), entry in zip(units, scores)
    ]
    lifted, norms = soft(scores)
    for (head, block), entry, norm in zip(units, lifted, norms):
        mixed = jnp.dot(entry, values[head], preferred_element_type=F32) / norm
        out_ref[block * BLOCK : (block + 1) * BLOCK, heads[head]] = mixed.astype(BF16)


def space_attend(where, mask, queries, own, other):
    rows, heads_width = queries.shape
    return pl.pallas_call(
        space_attend_kernel,
        in_specs=smem(2) + vmem(3),
        out_specs=vmem(1)[0],
        out_shape=jax.ShapeDtypeStruct((rows, heads_width), BF16),
        compiler_params=params(),
        cost_estimate=pl.CostEstimate(
            flops=8 * rows * rows * heads_width,
            bytes_accessed=12 * rows * heads_width,
            transcendentals=2 * rows * rows * heads_width // HD,
        ),
        name="space_attend",
    )(where, mask, queries, own, other)


def lend_kernel(where_ref, weight_ref, out_ref):
    groups, count, width = out_ref.shape
    lines = pl.ds(pl.multiple_of(where_ref[1] * count, 128), count)
    other_side = 1 - where_ref[2] % 2
    for group in range(groups):
        first = pl.multiple_of((2 * group + other_side) * width, 128)
        out_ref[group] = weight_ref[lines, pl.ds(first, width)]


def lend(where, weight, width):
    heads_width, model_width = weight.shape
    return pl.pallas_call(
        lend_kernel,
        in_specs=smem(1) + vmem(1),
        out_specs=vmem(1)[0],
        out_shape=jax.ShapeDtypeStruct((model_width // (2 * width), heads_width // 2, width), BF16),
        compiler_params=params(),
        cost_estimate=pl.CostEstimate(flops=0, bytes_accessed=2 * weight.size, transcendentals=0),
        name="lend",
    )(where, weight)


def project_kernel(where_ref, own_ref, partner_ref, weight_ref, half_ref, other_half_ref, out_ref, lent_ref):
    groups, _, width = out_ref.shape
    count = half_ref.shape[1]
    core, side = where_ref[1], where_ref[2] % 2
    lent_ref[:, pl.ds(pl.multiple_of(core * count, 128), count), :] = half_ref[...]
    lent_ref[:, pl.ds(pl.multiple_of((1 - core) * count, 128), count), :] = other_half_ref[...]
    for group in range(groups):
        first = pl.multiple_of((2 * group + side) * width, 128)
        product = jnp.dot(own_ref[...], weight_ref[:, pl.ds(first, width)], preferred_element_type=F32)
        product += jnp.dot(partner_ref[...], lent_ref[group], preferred_element_type=F32)
        out_ref[group] = product.astype(BF16)


def project(where, own, partner, weight, half, other_half):
    rows, heads_width = own.shape
    groups, _, width = half.shape
    return pl.pallas_call(
        project_kernel,
        in_specs=smem(1) + vmem(5),
        out_specs=vmem(1)[0],
        out_shape=jax.ShapeDtypeStruct((groups, rows, width), BF16),
        scratch_shapes=[pltpu.VMEM((groups, heads_width, width), BF16)],
        compiler_params=params(),
        cost_estimate=pl.CostEstimate(
            flops=4 * rows * heads_width * groups * width,
            bytes_accessed=2 * groups * width * (rows + 2 * heads_width),
            transcendentals=0,
        ),
        name="project",
    )(where, own, partner, weight, half, other_half)


def local_gate(where_ref, mod_ref, width):
    return mod_ref[2:3, pl.ds(pl.multiple_of(where_ref[2] * width, 128), width)]


def join_kernel(where_ref, parts_ref, tokens_ref, mod_ref, stream_ref, *sent_refs):
    total = parts_ref[0].astype(F32)
    for part in range(1, parts_ref.shape[0]):
        total += parts_ref[part].astype(F32)
    stream = tokens_ref[...] + local_gate(where_ref, mod_ref, total.shape[1]) * total
    stream_ref[...] = stream
    for sent_ref in sent_refs:
        sent_ref[...] = stream.astype(BF16)


def join(where, parts, tokens, mod, dtypes):
    count, rows, width = parts.shape
    return pl.pallas_call(
        join_kernel,
        in_specs=smem(1) + vmem(3),
        out_specs=vmem(len(dtypes)),
        out_shape=[jax.ShapeDtypeStruct((rows, width), dtype) for dtype in dtypes],
        compiler_params=params(),
        name="join",
    )(where, parts, tokens, mod)


def time_kernel(parts_ref, mod_ref, weight_ref, out_ref, normed_ref, packed_ref, att_ref):
    modulate(parts_ref, mod_ref, normed_ref)
    frames, places, heads_width = att_ref.shape
    for which, span, values in qkv_rows(normed_ref, weight_ref):
        first = span.start // places
        count = values.shape[0] // places
        packed_ref[which, first : first + count] = values.reshape(count, places, heads_width)
    group = 8
    span = frames * group
    row_place = lax.broadcasted_iota(jnp.int32, (span, span), 0) % group
    col_place = lax.broadcasted_iota(jnp.int32, (span, span), 1) % group
    bias = jnp.where(row_place == col_place, 0.0, -jnp.inf).astype(F32)
    units = [(start, low) for start in range(0, places, group) for low in range(0, heads_width, HD)]

    def chosen(which, start, low):
        block = packed_ref[which, :, start : start + group, low : low + HD]
        return block.reshape(span, HD).astype(BF16)

    scores = [against(chosen(0, *unit), chosen(1, *unit)) * SCALE + bias for unit in units]
    lifted, norms = soft(scores)
    for unit, entry, norm in zip(units, lifted, norms):
        mixed = jnp.dot(entry, chosen(2, *unit), preferred_element_type=F32) / norm
        start, low = unit
        att_ref[:, start : start + group, low : low + HD] = mixed.reshape(frames, group, HD)
    out_ref[...] = att_ref[...].reshape(frames * places, heads_width).astype(BF16)


def time_layer(parts, mod, weight, rows, frames):
    model_width, heads_width = weight.shape[1:]
    return pl.pallas_call(
        time_kernel,
        in_specs=vmem(3),
        out_specs=vmem(1)[0],
        out_shape=jax.ShapeDtypeStruct((rows, heads_width), BF16),
        scratch_shapes=[
            pltpu.VMEM((rows, model_width), BF16),
            pltpu.VMEM((3, frames, rows // frames, heads_width), F32),
            pltpu.VMEM((frames, rows // frames, heads_width), F32),
        ],
        compiler_params=params(),
        cost_estimate=pl.CostEstimate(
            flops=2 * rows * weight.size,
            bytes_accessed=2 * (weight.size + parts.size),
            transcendentals=rows * BLOCK * heads_width // HD,
        ),
        name="time_layer",
    )(parts, mod, weight)


def on_device(tokens, block_mask, space_qkv, space_out, space_mod, time_qkv, time_out, time_mod):
    videos, rows, width = tokens.shape
    parts = lax.axis_size("fsdp")
    seq_count = lax.axis_size("seq")
    frames = seq_count // 2
    seq_index = lax.axis_index("seq")
    where = jnp.stack([seq_index // 2, seq_index % 2, lax.axis_index("fsdp")]).astype(jnp.int32)
    same_half = [[2 * frame + half for frame in range(frames)] for half in range(2)]

    def across_frames(values):
        return lax.all_to_all(
            values.reshape(frames, rows // frames, -1), "seq", split_axis=0, concat_axis=0,
            tiled=True, axis_index_groups=same_half,
        ).reshape(rows, -1)

    def across_parts(values):
        return lax.all_to_all(values, "fsdp", split_axis=0, concat_axis=0, tiled=True)

    def gathered(shard):
        return across_parts(jnp.broadcast_to(shard[None], (parts,) + shard.shape))

    def from_other_core(values):
        return lax.ppermute(values, "seq", [(i, i ^ 1) for i in range(seq_count)])

    def from_other_side(values):
        return lax.ppermute(values, "fsdp", [(i, i ^ 1) for i in range(parts)])

    def projected(attended, weight, half):
        return project(
            where, attended, from_other_side(attended), weight, half, from_other_core(half)
        )

    def across_x(values):
        same_side = [[2 * group + side for group in range(parts // 2)] for side in range(2)]
        return lax.all_to_all(
            values, "fsdp", split_axis=0, concat_axis=0, tiled=True, axis_index_groups=same_side
        )

    local = tokens.reshape(rows, width)
    packed, lent = lax.optimization_barrier((pack(local), lend(where, space_out, width)))
    half = from_other_side(lent)
    queries, own = space_in(gathered(packed), space_mod, jnp.swapaxes(space_qkv, 0, 1), rows)
    attended = space_attend(where, block_mask.reshape(-1), queries, own, from_other_core(own))
    attended, time_weight = lax.optimization_barrier((attended, time_out))
    lent = lend(where, time_weight, width)
    partial, lent = lax.optimization_barrier((projected(attended, space_out, half), lent))
    half = from_other_side(lent)
    stream, sent = join(where, across_x(partial), local, space_mod, (F32, BF16))
    packed, half = lax.optimization_barrier((pack(across_frames(sent)), half))
    attended = time_layer(gathered(packed), time_mod, jnp.swapaxes(time_qkv, 0, 1), rows, frames)
    arrived = across_x(projected(across_frames(attended), time_out, half))
    return join(where, arrived, stream, time_mod, (F32,))[0].reshape(tokens.shape)


def solution(mesh):
    placed = (
        P(None, "seq", "fsdp"),
        P(),
        P(None, None, "fsdp"),
        P("fsdp", None),
        P(),
        P(None, None, "fsdp"),
        P("fsdp", None),
        P(),
    )
    return jax.shard_map(
        on_device, mesh=mesh, in_specs=placed, out_specs=P(None, "seq", "fsdp"), check_vma=False
    )
```

```python
import functools
import math

import jax
import jax.numpy as jnp
from jax import lax
from jax.experimental import pallas as pl
from jax.experimental.pallas import tpu as pltpu
from jax.sharding import PartitionSpec as P

HD = 128
BLOCK = 128
EPS = 1e-06
SCALE = 1.0 / math.sqrt(HD)
VMEM_LIMIT = 48 * 1024 * 1024
ROW_TILE = 192
F32 = jnp.float32
BF16 = jnp.bfloat16
STAT_ROWS = 8


def vmem(count):
    return [pl.BlockSpec(memory_space=pltpu.VMEM)] * count


def smem(count):
    return [pl.BlockSpec(memory_space=pltpu.SMEM)] * count


def params():
    return pltpu.CompilerParams(vmem_limit_bytes=VMEM_LIMIT)


def spread_columns(columns, rows):
    lane = lax.broadcasted_iota(jnp.int32, (rows, 128), 1)
    table = jnp.zeros((rows, 128), F32)
    for index, column in enumerate(columns):
        table = jnp.where(lane == index, column, table)
    return table


def bf16_terms(values, count):
    terms = []
    for _ in range(count):
        term = values.astype(BF16).astype(F32)
        terms.append(term)
        values = values - term
    return terms


def centre(values):
    mean = jnp.sum(values, axis=1, keepdims=True) / values.shape[1]
    centred = values - mean
    squares = jnp.sum(centred * centred, axis=1, keepdims=True)
    table = spread_columns(bf16_terms(mean, 3) + bf16_terms(squares, 2), values.shape[0])
    return centred.astype(BF16), table


def pack_kernel(tokens_ref, out_ref):
    rows = tokens_ref.shape[0]
    centred, table = centre(tokens_ref[...].astype(F32))
    out_ref[:rows, :] = centred
    out_ref[rows:, :] = jnp.transpose(table)[:STAT_ROWS].astype(BF16)


def pack(tokens):
    rows, width = tokens.shape
    shape = (rows + STAT_ROWS, width)
    return pl.pallas_call(
        pack_kernel,
        in_specs=vmem(1),
        out_specs=vmem(1)[0],
        out_shape=jax.ShapeDtypeStruct(shape, BF16),
        compiler_params=params(),
        name="pack",
    )(tokens)


def row_table(stats_ref, width):
    parts, _, rows = stats_ref.shape
    line = lax.broadcasted_iota(jnp.int32, (parts, rows), 0)
    means = jnp.zeros((parts, rows), F32)
    squares = 0.0
    for part in range(parts):
        lines = stats_ref[part].astype(F32)
        means = jnp.where(line == part, lines[0:1] + lines[1:2] + lines[2:3], means)
        squares = squares + (lines[3:4] + lines[4:5])
    offsets = means - jnp.sum(means, axis=0, keepdims=True) / parts
    between = jnp.sum(offsets * offsets, axis=0, keepdims=True) * width
    scale = lax.rsqrt((squares + between) / (parts * width) + EPS)
    scales = jnp.broadcast_to(scale, (128 - parts, rows))
    return jnp.transpose(jnp.concatenate([offsets, scales], axis=0))


def modulate(parts_ref, mod_ref, normed_ref):
    parts, total_rows, width = parts_ref.shape
    rows = normed_ref.shape[0]
    table = row_table(parts_ref.at[:, rows:total_rows, :], width)
    scale = jnp.broadcast_to(table[:, 127:128], (rows, 128))
    for part in range(parts):
        offset = jnp.broadcast_to(table[:, part : part + 1], (rows, 128))
        for start in range(0, width, 128):
            columns = slice(part * width + start, part * width + start + 128)
            values = parts_ref[part, :rows, start : start + 128].astype(F32)
            gain = 1.0 + mod_ref[1:2, columns]
            normed_ref[:, columns] = (
                ((values + offset) * scale) * gain + mod_ref[0:1, columns]
            ).astype(BF16)


def qkv_rows(parts_ref, mod_ref, weight_ref, normed_ref, held_ref, done):
    copies = [
        pltpu.make_async_copy(weight_ref.at[which], held_ref.at[which], done.at[which])
        for which in range(3)
    ]
    for copy in copies:
        copy.start()
    modulate(parts_ref, mod_ref, normed_ref)
    rows = normed_ref.shape[0]
    tile = ROW_TILE if rows % ROW_TILE == 0 else rows
    for which in range(3):
        copies[which].wait()
        for start in range(0, rows, tile):
            span = slice(start, start + tile)
            yield which, span, jnp.dot(
                normed_ref[span, :], held_ref[which], preferred_element_type=F32
            )


def qkv_operands(rows, weight):
    specs = vmem(2) + [pl.BlockSpec(memory_space=pl.ANY)]
    scratch = [
        pltpu.VMEM((rows, weight.shape[1]), BF16),
        pltpu.VMEM(weight.shape, BF16),
        pltpu.SemaphoreType.DMA((3,)),
    ]
    return specs, scratch


def space_in_kernel(parts_ref, mod_ref, weight_ref, q_ref, kv_ref, *scratch):
    for which, span, values in qkv_rows(parts_ref, mod_ref, weight_ref, *scratch):
        if which == 0:
            q_ref[span, :] = values.astype(BF16)
        else:
            kv_ref[which - 1, span, :] = values.astype(BF16)


def space_in(parts, mod, weight, rows):
    heads_width = weight.shape[2]
    specs, scratch = qkv_operands(rows, weight)
    return pl.pallas_call(
        space_in_kernel,
        in_specs=specs,
        out_specs=vmem(2),
        out_shape=[
            jax.ShapeDtypeStruct((rows, heads_width), BF16),
            jax.ShapeDtypeStruct((2, rows, heads_width), BF16),
        ],
        scratch_shapes=scratch,
        compiler_params=params(),
        cost_estimate=pl.CostEstimate(
            flops=2 * rows * weight.size,
            bytes_accessed=2 * (weight.size + parts.size),
            transcendentals=0,
        ),
        name="space_in",
    )(parts, mod, weight)


def soft(scores):
    lifted = [jnp.exp(entry - jnp.max(entry, axis=1, keepdims=True)) for entry in scores]
    norms = [jnp.sum(entry, axis=1, keepdims=True) for entry in lifted]
    return [entry.astype(BF16) for entry in lifted], norms


def against(query, keys):
    return lax.dot_general(query, keys, (((1,), (1,)), ((), ())), preferred_element_type=F32)


def space_attend_kernel(where_ref, mask_ref, q_ref, own_ref, other_ref, out_ref):
    rows, heads_width = q_ref.shape
    query_blocks = rows // BLOCK
    key_blocks = 2 * query_blocks
    half = where_ref[1]
    mask_base = (where_ref[0] * key_blocks + half * query_blocks) * key_blocks
    biases = []
    for block in range(query_blocks):
        line = []
        for side in range(2):
            first = (half if side == 0 else 1 - half) * query_blocks
            for key_block in range(query_blocks):
                kept = mask_ref[mask_base + block * key_blocks + first + key_block]
                line.append(jnp.where(kept == 1, 0.0, -jnp.inf).astype(F32))
        biases.append(line)
    heads = [slice(start, start + HD) for start in range(0, heads_width, HD)]
    keys = [jnp.concatenate([own_ref[0, :, head], other_ref[0, :, head]], axis=0) for head in heads]
    values = [jnp.concatenate([own_ref[1, :, head], other_ref[1, :, head]], axis=0) for head in heads]
    units = [(head, block) for head in range(len(heads)) for block in range(query_blocks)]
    scores = [
        against(q_ref[block * BLOCK : (block + 1) * BLOCK, heads[head]], keys[head])
        for head, block in units
    ]
    scores = [
        jnp.concatenate(
            [
                entry[:, index * BLOCK : (index + 1) * BLOCK] * SCALE + bias
                for index, bias in enumerate(biases[block])
            ],
            axis=1,
        )
        for (_, block), entry in zip(units, scores)
    ]
    lifted, norms = soft(scores)
    for (head, block), entry, norm in zip(units, lifted, norms):
        mixed = jnp.dot(entry, values[head], preferred_element_type=F32) / norm
        out_ref[block * BLOCK : (block + 1) * BLOCK, heads[head]] = mixed.astype(BF16)


def space_attend(where, mask, queries, own, other):
    rows, heads_width = queries.shape
    return pl.pallas_call(
        space_attend_kernel,
        in_specs=smem(2) + vmem(3),
        out_specs=vmem(1)[0],
        out_shape=jax.ShapeDtypeStruct((rows, heads_width), BF16),
        compiler_params=params(),
        cost_estimate=pl.CostEstimate(
            flops=8 * rows * rows * heads_width,
            bytes_accessed=12 * rows * heads_width,
            transcendentals=2 * rows * rows * heads_width // HD,
        ),
        name="space_attend",
    )(where, mask, queries, own, other)


def lend_kernel(where_ref, *refs):
    layers = (len(refs) - 1) // 2
    done = refs[-1]
    copies = []
    for weight_ref, out_ref in zip(refs[:layers], refs[layers : 2 * layers]):
        groups, count, width = out_ref.shape
        lines = pl.ds(pl.multiple_of(where_ref[1] * count, 128), count)
        other_side = 1 - where_ref[2] % 2
        for group in range(groups):
            first = pl.multiple_of((2 * group + other_side) * width, 128)
            copies.append(
                pltpu.make_async_copy(
                    weight_ref.at[lines, pl.ds(first, width)], out_ref.at[group], done.at[len(copies)]
                )
            )
    for copy in copies:
        copy.start()
    for copy in copies:
        copy.wait()


def lend(where, weights, width):
    heads_width, model_width = weights[0].shape
    groups = model_width // (2 * width)
    shape = jax.ShapeDtypeStruct((groups, heads_width // 2, width), BF16)
    return pl.pallas_call(
        lend_kernel,
        in_specs=smem(1) + [pl.BlockSpec(memory_space=pl.ANY)] * len(weights),
        out_specs=vmem(len(weights)),
        out_shape=[shape] * len(weights),
        scratch_shapes=[pltpu.SemaphoreType.DMA((groups * len(weights),))],
        compiler_params=params(),
        cost_estimate=pl.CostEstimate(
            flops=0, bytes_accessed=2 * len(weights) * weights[0].size, transcendentals=0
        ),
        name="lend",
    )(where, *weights)


def project_kernel(where_ref, own_ref, partner_ref, weight_ref, half_ref, other_half_ref, out_ref, lent_ref):
    groups, _, width = out_ref.shape
    count = half_ref.shape[1]
    core, side = where_ref[1], where_ref[2] % 2
    lent_ref[:, pl.ds(pl.multiple_of(core * count, 128), count), :] = half_ref[...]
    lent_ref[:, pl.ds(pl.multiple_of((1 - core) * count, 128), count), :] = other_half_ref[...]
    for group in range(groups):
        first = pl.multiple_of((2 * group + side) * width, 128)
        product = jnp.dot(own_ref[...], weight_ref[:, pl.ds(first, width)], preferred_element_type=F32)
        product += jnp.dot(partner_ref[...], lent_ref[group], preferred_element_type=F32)
        out_ref[group] = product.astype(BF16)


def project(where, own, partner, weight, half, other_half):
    rows, heads_width = own.shape
    groups, _, width = half.shape
    return pl.pallas_call(
        project_kernel,
        in_specs=smem(1) + vmem(5),
        out_specs=vmem(1)[0],
        out_shape=jax.ShapeDtypeStruct((groups, rows, width), BF16),
        scratch_shapes=[pltpu.VMEM((groups, heads_width, width), BF16)],
        compiler_params=params(),
        cost_estimate=pl.CostEstimate(
            flops=4 * rows * heads_width * groups * width,
            bytes_accessed=2 * groups * width * (rows + 2 * heads_width),
            transcendentals=0,
        ),
        name="project",
    )(where, own, partner, weight, half, other_half)


def local_gate(where_ref, mod_ref, width):
    return mod_ref[2:3, pl.ds(pl.multiple_of(where_ref[2] * width, 128), width)]


def join_kernel(where_ref, parts_ref, tokens_ref, mod_ref, stream_ref, *sent_refs):
    total = parts_ref[0].astype(F32)
    for part in range(1, parts_ref.shape[0]):
        total += parts_ref[part].astype(F32)
    stream = tokens_ref[...] + local_gate(where_ref, mod_ref, total.shape[1]) * total
    stream_ref[...] = stream
    for sent_ref in sent_refs:
        sent_ref[...] = stream.astype(BF16)


def join(where, parts, tokens, mod, dtypes):
    count, rows, width = parts.shape
    return pl.pallas_call(
        join_kernel,
        in_specs=smem(1) + vmem(3),
        out_specs=vmem(len(dtypes)),
        out_shape=[jax.ShapeDtypeStruct((rows, width), dtype) for dtype in dtypes],
        compiler_params=params(),
        name="join",
    )(where, parts, tokens, mod)


def time_kernel(parts_ref, mod_ref, weight_ref, out_ref, packed_ref, att_ref, *scratch):
    frames, places, heads_width = att_ref.shape
    for which, span, values in qkv_rows(parts_ref, mod_ref, weight_ref, *scratch):
        first = span.start // places
        count = values.shape[0] // places
        packed_ref[which, first : first + count] = values.reshape(count, places, heads_width)
    group = 8
    span = frames * group
    row_place = lax.broadcasted_iota(jnp.int32, (span, span), 0) % group
    col_place = lax.broadcasted_iota(jnp.int32, (span, span), 1) % group
    bias = jnp.where(row_place == col_place, 0.0, -jnp.inf).astype(F32)
    units = [(start, low) for start in range(0, places, group) for low in range(0, heads_width, HD)]

    def chosen(which, start, low):
        block = packed_ref[which, :, start : start + group, low : low + HD]
        return block.reshape(span, HD).astype(BF16)

    scores = [against(chosen(0, *unit), chosen(1, *unit)) * SCALE + bias for unit in units]
    lifted, norms = soft(scores)
    for unit, entry, norm in zip(units, lifted, norms):
        mixed = jnp.dot(entry, chosen(2, *unit), preferred_element_type=F32) / norm
        start, low = unit
        att_ref[:, start : start + group, low : low + HD] = mixed.reshape(frames, group, HD)
    out_ref[...] = att_ref[...].reshape(frames * places, heads_width).astype(BF16)


def time_layer(parts, mod, weight, rows, frames):
    heads_width = weight.shape[2]
    specs, scratch = qkv_operands(rows, weight)
    return pl.pallas_call(
        time_kernel,
        in_specs=specs,
        out_specs=vmem(1)[0],
        out_shape=jax.ShapeDtypeStruct((rows, heads_width), BF16),
        scratch_shapes=[
            pltpu.VMEM((3, frames, rows // frames, heads_width), F32),
            pltpu.VMEM((frames, rows // frames, heads_width), F32),
        ]
        + scratch,
        compiler_params=params(),
        cost_estimate=pl.CostEstimate(
            flops=2 * rows * weight.size,
            bytes_accessed=2 * (weight.size + parts.size),
            transcendentals=rows * BLOCK * heads_width // HD,
        ),
        name="time_layer",
    )(parts, mod, weight)


def on_device(tokens, block_mask, space_qkv, space_out, space_mod, time_qkv, time_out, time_mod):
    videos, rows, width = tokens.shape
    parts = lax.axis_size("fsdp")
    seq_count = lax.axis_size("seq")
    frames = seq_count // 2
    seq_index = lax.axis_index("seq")
    where = jnp.stack([seq_index // 2, seq_index % 2, lax.axis_index("fsdp")]).astype(jnp.int32)
    same_half = [[2 * frame + half for frame in range(frames)] for half in range(2)]

    def across_frames(values):
        return lax.all_to_all(
            values.reshape(frames, rows // frames, -1), "seq", split_axis=0, concat_axis=0,
            tiled=True, axis_index_groups=same_half,
        ).reshape(rows, -1)

    def across_parts(values):
        return lax.all_to_all(values, "fsdp", split_axis=0, concat_axis=0, tiled=True)

    def gathered(shard):
        return across_parts(jnp.broadcast_to(shard[None], (parts,) + shard.shape))

    def from_other_core(values):
        return lax.ppermute(values, "seq", [(i, i ^ 1) for i in range(seq_count)])

    def from_other_side(values):
        return lax.ppermute(values, "fsdp", [(i, i ^ 1) for i in range(parts)])

    def projected(attended, weight, half):
        return project(
            where, attended, from_other_side(attended), weight, half, from_other_core(half)
        )

    def across_x(values):
        same_side = [[2 * group + side for group in range(parts // 2)] for side in range(2)]
        return lax.all_to_all(
            values, "fsdp", split_axis=0, concat_axis=0, tiled=True, axis_index_groups=same_side
        )

    local = tokens.reshape(rows, width)
    space_lent, time_lent = lend(where, (space_out, time_out), width)
    half = from_other_side(space_lent)
    queries, own = space_in(gathered(pack(local)), space_mod, jnp.swapaxes(space_qkv, 0, 1), rows)
    attended = space_attend(where, block_mask.reshape(-1), queries, own, from_other_core(own))
    partial = projected(attended, space_out, half)
    partial, time_lent = lax.optimization_barrier((partial, time_lent))
    half = from_other_side(time_lent)
    stream, sent = join(where, across_x(partial), local, space_mod, (F32, BF16))
    sent, half = lax.optimization_barrier((sent, half))
    wide = gathered(pack(across_frames(sent)))
    attended = time_layer(wide, time_mod, jnp.swapaxes(time_qkv, 0, 1), rows, frames)
    arrived = across_x(projected(across_frames(attended), time_out, half))
    return join(where, arrived, stream, time_mod, (F32,))[0].reshape(tokens.shape)


def solution(mesh):
    placed = (
        P(None, "seq", "fsdp"),
        P(),
        P(None, None, "fsdp"),
        P("fsdp", None),
        P(),
        P(None, None, "fsdp"),
        P("fsdp", None),
        P(),
    )
    return jax.shard_map(
        on_device, mesh=mesh, in_specs=placed, out_specs=P(None, "seq", "fsdp"), check_vma=False
    )
```

```python
import functools
import math

import jax
import jax.numpy as jnp
from jax import lax
from jax.experimental import pallas as pl
from jax.experimental.pallas import tpu as pltpu
from jax.sharding import PartitionSpec as P

HD = 128
BLOCK = 128
EPS = 1e-06
SCALE = 1.0 / math.sqrt(HD)
VMEM_LIMIT = 24 * 1024 * 1024
HELD_LIMIT = 52 * 1024 * 1024
ROW_TILE = 192
F32 = jnp.float32
BF16 = jnp.bfloat16
STAT_ROWS = 8


def vmem(count):
    return [pl.BlockSpec(memory_space=pltpu.VMEM)] * count


def smem(count):
    return [pl.BlockSpec(memory_space=pltpu.SMEM)] * count


def params(limit=None):
    return pltpu.CompilerParams(vmem_limit_bytes=limit or VMEM_LIMIT)


def spread_columns(columns, rows):
    lane = lax.broadcasted_iota(jnp.int32, (rows, 128), 1)
    table = jnp.zeros((rows, 128), F32)
    for index, column in enumerate(columns):
        table = jnp.where(lane == index, column, table)
    return table


def bf16_terms(values, count):
    terms = []
    for _ in range(count):
        term = values.astype(BF16).astype(F32)
        terms.append(term)
        values = values - term
    return terms


def centre(values):
    mean = jnp.sum(values, axis=1, keepdims=True) / values.shape[1]
    centred = values - mean
    squares = jnp.sum(centred * centred, axis=1, keepdims=True)
    table = spread_columns(bf16_terms(mean, 3) + bf16_terms(squares, 2), values.shape[0])
    return centred.astype(BF16), table


def pack_kernel(tokens_ref, out_ref):
    rows = tokens_ref.shape[0]
    centred, table = centre(tokens_ref[...].astype(F32))
    out_ref[:rows, :] = centred
    out_ref[rows:, :] = jnp.transpose(table)[:STAT_ROWS].astype(BF16)


def pack(tokens):
    rows, width = tokens.shape
    shape = (rows + STAT_ROWS, width)
    return pl.pallas_call(
        pack_kernel,
        in_specs=vmem(1),
        out_specs=vmem(1)[0],
        out_shape=jax.ShapeDtypeStruct(shape, BF16),
        compiler_params=params(),
        name="pack",
    )(tokens)


def row_table(stats_ref, width):
    parts, _, rows = stats_ref.shape
    line = lax.broadcasted_iota(jnp.int32, (parts, rows), 0)
    means = jnp.zeros((parts, rows), F32)
    squares = 0.0
    for part in range(parts):
        lines = stats_ref[part].astype(F32)
        means = jnp.where(line == part, lines[0:1] + lines[1:2] + lines[2:3], means)
        squares = squares + (lines[3:4] + lines[4:5])
    offsets = means - jnp.sum(means, axis=0, keepdims=True) / parts
    between = jnp.sum(offsets * offsets, axis=0, keepdims=True) * width
    scale = lax.rsqrt((squares + between) / (parts * width) + EPS)
    scales = jnp.broadcast_to(scale, (128 - parts, rows))
    return jnp.transpose(jnp.concatenate([offsets, scales], axis=0))


def modulate(parts_ref, mod_ref, normed_ref, copies):
    parts, total_rows, width = parts_ref.shape
    rows = normed_ref.shape[0]
    table = row_table(parts_ref.at[:, rows:total_rows, :], width)
    scale = jnp.broadcast_to(table[:, 127:128], (rows, 128))
    for part in range(parts):
        if copies and part in (parts // 4, parts // 2):
            copies[part // (parts // 4) - 1].start()
        offset = jnp.broadcast_to(table[:, part : part + 1], (rows, 128))
        for start in range(0, width, 128):
            columns = slice(part * width + start, part * width + start + 128)
            values = parts_ref[part, :rows, start : start + 128].astype(F32)
            gain = 1.0 + mod_ref[1:2, columns]
            normed_ref[:, columns] = (
                ((values + offset) * scale) * gain + mod_ref[0:1, columns]
            ).astype(BF16)


def qkv_rows(parts_ref, mod_ref, weight_ref, normed_ref, held_ref=None, done=None):
    copies = []
    if held_ref is not None:
        copies = [
            pltpu.make_async_copy(weight_ref.at[which], held_ref.at[which], done.at[which])
            for which in range(3)
        ]
        copies[0].start()
        weight_ref = held_ref
    modulate(parts_ref, mod_ref, normed_ref, copies[1:])
    rows = normed_ref.shape[0]
    tile = ROW_TILE if rows % ROW_TILE == 0 else rows
    for which in range(3):
        if copies:
            copies[which].wait()
        for start in range(0, rows, tile):
            span = slice(start, start + tile)
            yield which, span, jnp.dot(
                normed_ref[span, :], weight_ref[which], preferred_element_type=F32
            )


def space_in_kernel(parts_ref, mod_ref, weight_ref, q_ref, kv_ref, *scratch):
    for which, span, values in qkv_rows(parts_ref, mod_ref, weight_ref, *scratch):
        if which == 0:
            q_ref[span, :] = values.astype(BF16)
        else:
            kv_ref[which - 1, span, :] = values.astype(BF16)


def space_in(parts, mod, weight, rows):
    heads_width = weight.shape[2]
    return pl.pallas_call(
        space_in_kernel,
        in_specs=vmem(2) + [pl.BlockSpec(memory_space=pl.ANY)],
        out_specs=vmem(2),
        out_shape=[
            jax.ShapeDtypeStruct((rows, heads_width), BF16),
            jax.ShapeDtypeStruct((2, rows, heads_width), BF16),
        ],
        scratch_shapes=[
            pltpu.VMEM((rows, weight.shape[1]), BF16),
            pltpu.VMEM(weight.shape, BF16),
            pltpu.SemaphoreType.DMA((3,)),
        ],
        compiler_params=params(HELD_LIMIT),
        cost_estimate=pl.CostEstimate(
            flops=2 * rows * weight.size,
            bytes_accessed=2 * (weight.size + parts.size),
            transcendentals=0,
        ),
        name="space_in",
    )(parts, mod, weight)


def soft(scores):
    lifted = [jnp.exp(entry - jnp.max(entry, axis=1, keepdims=True)) for entry in scores]
    norms = [jnp.sum(entry, axis=1, keepdims=True) for entry in lifted]
    return [entry.astype(BF16) for entry in lifted], norms


def against(query, keys):
    return lax.dot_general(query, keys, (((1,), (1,)), ((), ())), preferred_element_type=F32)


def space_attend_kernel(where_ref, mask_ref, q_ref, own_ref, other_ref, out_ref):
    rows, heads_width = q_ref.shape
    query_blocks = rows // BLOCK
    key_blocks = 2 * query_blocks
    half = where_ref[1]
    mask_base = (where_ref[0] * key_blocks + half * query_blocks) * key_blocks
    biases = []
    for block in range(query_blocks):
        line = []
        for side in range(2):
            first = (half if side == 0 else 1 - half) * query_blocks
            for key_block in range(query_blocks):
                kept = mask_ref[mask_base + block * key_blocks + first + key_block]
                line.append(jnp.where(kept == 1, 0.0, -jnp.inf).astype(F32))
        biases.append(line)
    heads = [slice(start, start + HD) for start in range(0, heads_width, HD)]
    keys = [jnp.concatenate([own_ref[0, :, head], other_ref[0, :, head]], axis=0) for head in heads]
    values = [jnp.concatenate([own_ref[1, :, head], other_ref[1, :, head]], axis=0) for head in heads]
    units = [(head, block) for head in range(len(heads)) for block in range(query_blocks)]
    scores = [
        against(q_ref[block * BLOCK : (block + 1) * BLOCK, heads[head]], keys[head])
        for head, block in units
    ]
    scores = [
        jnp.concatenate(
            [
                entry[:, index * BLOCK : (index + 1) * BLOCK] * SCALE + bias
                for index, bias in enumerate(biases[block])
            ],
            axis=1,
        )
        for (_, block), entry in zip(units, scores)
    ]
    lifted, norms = soft(scores)
    for (head, block), entry, norm in zip(units, lifted, norms):
        mixed = jnp.dot(entry, values[head], preferred_element_type=F32) / norm
        out_ref[block * BLOCK : (block + 1) * BLOCK, heads[head]] = mixed.astype(BF16)


def space_attend(where, mask, queries, own, other):
    rows, heads_width = queries.shape
    return pl.pallas_call(
        space_attend_kernel,
        in_specs=smem(2) + vmem(3),
        out_specs=vmem(1)[0],
        out_shape=jax.ShapeDtypeStruct((rows, heads_width), BF16),
        compiler_params=params(),
        cost_estimate=pl.CostEstimate(
            flops=8 * rows * rows * heads_width,
            bytes_accessed=12 * rows * heads_width,
            transcendentals=2 * rows * rows * heads_width // HD,
        ),
        name="space_attend",
    )(where, mask, queries, own, other)


def lend_kernel(where_ref, *refs):
    layers = (len(refs) - 1) // 3
    done = refs[-1]
    side = where_ref[2] % 2
    copies = []
    for layer in range(layers):
        weight_ref, lent_ref, kept_ref = refs[layer], refs[layers + layer], refs[2 * layers + layer]
        groups, count, width = lent_ref.shape
        lines = pl.ds(pl.multiple_of(where_ref[1] * count, 128), count)
        for group in range(groups):
            there = pl.ds(pl.multiple_of((2 * group + 1 - side) * width, 128), width)
            here = pl.ds(pl.multiple_of((2 * group + side) * width, 128), width)
            copies.append((weight_ref.at[lines, there], lent_ref.at[group]))
            copies.append((weight_ref.at[:, here], kept_ref.at[group]))
    copies = [
        pltpu.make_async_copy(source, target, done.at[index])
        for index, (source, target) in enumerate(copies)
    ]
    for copy in copies:
        copy.start()
    for copy in copies:
        copy.wait()


def lend(where, weights, width):
    layers = len(weights)
    heads_width, model_width = weights[0].shape
    groups = model_width // (2 * width)
    lent = jax.ShapeDtypeStruct((groups, heads_width // 2, width), BF16)
    kept = jax.ShapeDtypeStruct((groups, heads_width, width), BF16)
    outs = pl.pallas_call(
        lend_kernel,
        in_specs=smem(1) + [pl.BlockSpec(memory_space=pl.ANY)] * layers,
        out_specs=vmem(2 * layers),
        out_shape=[lent] * layers + [kept] * layers,
        scratch_shapes=[pltpu.SemaphoreType.DMA((2 * groups * layers,))],
        compiler_params=params(),
        cost_estimate=pl.CostEstimate(
            flops=0, bytes_accessed=3 * layers * weights[0].size, transcendentals=0
        ),
        name="lend",
    )(where, *weights)
    return outs[:layers], outs[layers:]


def project_kernel(where_ref, own_ref, partner_ref, weight_ref, half_ref, other_half_ref, out_ref, lent_ref):
    groups = out_ref.shape[0]
    count = half_ref.shape[1]
    core = where_ref[1]
    lent_ref[:, pl.ds(pl.multiple_of(core * count, 128), count), :] = half_ref[...]
    lent_ref[:, pl.ds(pl.multiple_of((1 - core) * count, 128), count), :] = other_half_ref[...]
    for group in range(groups):
        product = jnp.dot(own_ref[...], weight_ref[group], preferred_element_type=F32)
        product += jnp.dot(partner_ref[...], lent_ref[group], preferred_element_type=F32)
        out_ref[group] = product.astype(BF16)


def project(where, own, partner, weight, half, other_half):
    rows, heads_width = own.shape
    groups, _, width = half.shape
    return pl.pallas_call(
        project_kernel,
        in_specs=smem(1) + vmem(5),
        out_specs=vmem(1)[0],
        out_shape=jax.ShapeDtypeStruct((groups, rows, width), BF16),
        scratch_shapes=[pltpu.VMEM((groups, heads_width, width), BF16)],
        compiler_params=params(),
        cost_estimate=pl.CostEstimate(
            flops=4 * rows * heads_width * groups * width,
            bytes_accessed=2 * groups * width * (rows + 2 * heads_width),
            transcendentals=0,
        ),
        name="project",
    )(where, own, partner, weight, half, other_half)


def local_gate(where_ref, mod_ref, width):
    return mod_ref[2:3, pl.ds(pl.multiple_of(where_ref[2] * width, 128), width)]


def join_kernel(where_ref, parts_ref, tokens_ref, mod_ref, stream_ref, *sent_refs):
    total = parts_ref[0].astype(F32)
    for part in range(1, parts_ref.shape[0]):
        total += parts_ref[part].astype(F32)
    stream = tokens_ref[...] + local_gate(where_ref, mod_ref, total.shape[1]) * total
    stream_ref[...] = stream
    for sent_ref in sent_refs:
        sent_ref[...] = stream.astype(BF16)


def join(where, parts, tokens, mod, dtypes):
    count, rows, width = parts.shape
    return pl.pallas_call(
        join_kernel,
        in_specs=smem(1) + vmem(3),
        out_specs=vmem(len(dtypes)),
        out_shape=[jax.ShapeDtypeStruct((rows, width), dtype) for dtype in dtypes],
        compiler_params=params(),
        name="join",
    )(where, parts, tokens, mod)


def time_kernel(parts_ref, mod_ref, weight_ref, out_ref, packed_ref, att_ref, *scratch):
    frames, places, heads_width = att_ref.shape
    for which, span, values in qkv_rows(parts_ref, mod_ref, weight_ref, *scratch):
        first = span.start // places
        count = values.shape[0] // places
        packed_ref[which, first : first + count] = values.reshape(count, places, heads_width)
    group = 8
    span = frames * group
    row_place = lax.broadcasted_iota(jnp.int32, (span, span), 0) % group
    col_place = lax.broadcasted_iota(jnp.int32, (span, span), 1) % group
    bias = jnp.where(row_place == col_place, 0.0, -jnp.inf).astype(F32)
    units = [(start, low) for start in range(0, places, group) for low in range(0, heads_width, HD)]

    def chosen(which, start, low):
        block = packed_ref[which, :, start : start + group, low : low + HD]
        return block.reshape(span, HD).astype(BF16)

    scores = [against(chosen(0, *unit), chosen(1, *unit)) * SCALE + bias for unit in units]
    lifted, norms = soft(scores)
    for unit, entry, norm in zip(units, lifted, norms):
        mixed = jnp.dot(entry, chosen(2, *unit), preferred_element_type=F32) / norm
        start, low = unit
        att_ref[:, start : start + group, low : low + HD] = mixed.reshape(frames, group, HD)
    out_ref[...] = att_ref[...].reshape(frames * places, heads_width).astype(BF16)


def time_layer(parts, mod, weight, rows, frames):
    heads_width = weight.shape[2]
    return pl.pallas_call(
        time_kernel,
        in_specs=vmem(3),
        out_specs=vmem(1)[0],
        out_shape=jax.ShapeDtypeStruct((rows, heads_width), BF16),
        scratch_shapes=[
            pltpu.VMEM((3, frames, rows // frames, heads_width), F32),
            pltpu.VMEM((frames, rows // frames, heads_width), F32),
            pltpu.VMEM((rows, weight.shape[1]), BF16),
        ],
        compiler_params=params(),
        cost_estimate=pl.CostEstimate(
            flops=2 * rows * weight.size,
            bytes_accessed=2 * (weight.size + parts.size),
            transcendentals=rows * BLOCK * heads_width // HD,
        ),
        name="time_layer",
    )(parts, mod, weight)


def on_device(tokens, block_mask, space_qkv, space_out, space_mod, time_qkv, time_out, time_mod):
    videos, rows, width = tokens.shape
    parts = lax.axis_size("fsdp")
    seq_count = lax.axis_size("seq")
    frames = seq_count // 2
    seq_index = lax.axis_index("seq")
    where = jnp.stack([seq_index // 2, seq_index % 2, lax.axis_index("fsdp")]).astype(jnp.int32)
    same_half = [[2 * frame + half for frame in range(frames)] for half in range(2)]

    def across_frames(values):
        return lax.all_to_all(
            values.reshape(frames, rows // frames, -1), "seq", split_axis=0, concat_axis=0,
            tiled=True, axis_index_groups=same_half,
        ).reshape(rows, -1)

    def across_parts(values):
        return lax.all_to_all(values, "fsdp", split_axis=0, concat_axis=0, tiled=True)

    def gathered(shard):
        return across_parts(jnp.broadcast_to(shard[None], (parts,) + shard.shape))

    def from_other_core(values):
        return lax.ppermute(values, "seq", [(i, i ^ 1) for i in range(seq_count)])

    def from_other_side(values):
        return lax.ppermute(values, "fsdp", [(i, i ^ 1) for i in range(parts)])

    def projected(attended, weight, half):
        return project(
            where, attended, from_other_side(attended), weight, half, from_other_core(half)
        )

    def across_x(values):
        same_side = [[2 * group + side for group in range(parts // 2)] for side in range(2)]
        return lax.all_to_all(
            values, "fsdp", split_axis=0, concat_axis=0, tiled=True, axis_index_groups=same_side
        )

    local = tokens.reshape(rows, width)
    (space_lent, time_lent), (space_kept, time_kept) = lend(where, (space_out, time_out), width)
    half = from_other_side(space_lent)
    queries, own = space_in(gathered(pack(local)), space_mod, jnp.swapaxes(space_qkv, 0, 1), rows)
    attended = space_attend(where, block_mask.reshape(-1), queries, own, from_other_core(own))
    partial = projected(attended, space_kept, half)
    partial, time_lent = lax.optimization_barrier((partial, time_lent))
    half = from_other_side(time_lent)
    stream, sent = join(where, across_x(partial), local, space_mod, (F32, BF16))
    sent, half = lax.optimization_barrier((sent, half))
    wide = gathered(pack(across_frames(sent)))
    attended = time_layer(wide, time_mod, jnp.swapaxes(time_qkv, 0, 1), rows, frames)
    arrived = across_x(projected(across_frames(attended), time_kept, half))
    return join(where, arrived, stream, time_mod, (F32,))[0].reshape(tokens.shape)


def solution(mesh):
    placed = (
        P(None, "seq", "fsdp"),
        P(),
        P(None, None, "fsdp"),
        P("fsdp", None),
        P(),
        P(None, None, "fsdp"),
        P("fsdp", None),
        P(),
    )
    return jax.shard_map(
        on_device, mesh=mesh, in_specs=placed, out_specs=P(None, "seq", "fsdp"), check_vma=False
    )
```

```python
import functools
import math

import jax
import jax.numpy as jnp
from jax import lax
from jax.experimental import pallas as pl
from jax.experimental.pallas import tpu as pltpu
from jax.sharding import PartitionSpec as P

HD = 128
BLOCK = 128
EPS = 1e-06
SCALE = 1.0 / math.sqrt(HD)
VMEM_LIMIT = 24 * 1024 * 1024
HELD_LIMIT = 52 * 1024 * 1024
ROW_TILE = 192
F32 = jnp.float32
BF16 = jnp.bfloat16
STAT_ROWS = 8


def vmem(count):
    return [pl.BlockSpec(memory_space=pltpu.VMEM)] * count


def smem(count):
    return [pl.BlockSpec(memory_space=pltpu.SMEM)] * count


def params(limit=None):
    return pltpu.CompilerParams(vmem_limit_bytes=limit or VMEM_LIMIT)


def spread_columns(columns, rows):
    lane = lax.broadcasted_iota(jnp.int32, (rows, 128), 1)
    table = jnp.zeros((rows, 128), F32)
    for index, column in enumerate(columns):
        table = jnp.where(lane == index, column, table)
    return table


def bf16_terms(values, count):
    terms = []
    for _ in range(count):
        term = values.astype(BF16).astype(F32)
        terms.append(term)
        values = values - term
    return terms


def centre(values):
    mean = jnp.sum(values, axis=1, keepdims=True) / values.shape[1]
    centred = values - mean
    squares = jnp.sum(centred * centred, axis=1, keepdims=True)
    table = spread_columns(bf16_terms(mean, 3) + bf16_terms(squares, 2), values.shape[0])
    return centred.astype(BF16), table


def pack_kernel(tokens_ref, out_ref):
    rows = tokens_ref.shape[0]
    centred, table = centre(tokens_ref[...].astype(F32))
    out_ref[:rows, :] = centred
    out_ref[rows:, :] = jnp.transpose(table)[:STAT_ROWS].astype(BF16)


def pack(tokens):
    rows, width = tokens.shape
    shape = (rows + STAT_ROWS, width)
    return pl.pallas_call(
        pack_kernel,
        in_specs=vmem(1),
        out_specs=vmem(1)[0],
        out_shape=jax.ShapeDtypeStruct(shape, BF16),
        compiler_params=params(),
        name="pack",
    )(tokens)


def row_table(stats_ref, width):
    parts, _, rows = stats_ref.shape
    line = lax.broadcasted_iota(jnp.int32, (parts, rows), 0)
    means = jnp.zeros((parts, rows), F32)
    squares = 0.0
    for part in range(parts):
        lines = stats_ref[part].astype(F32)
        means = jnp.where(line == part, lines[0:1] + lines[1:2] + lines[2:3], means)
        squares = squares + (lines[3:4] + lines[4:5])
    offsets = means - jnp.sum(means, axis=0, keepdims=True) / parts
    between = jnp.sum(offsets * offsets, axis=0, keepdims=True) * width
    scale = lax.rsqrt((squares + between) / (parts * width) + EPS)
    scales = jnp.broadcast_to(scale, (128 - parts, rows))
    return jnp.transpose(jnp.concatenate([offsets, scales], axis=0))


def modulate(parts_ref, mod_ref, normed_ref):
    parts, total_rows, width = parts_ref.shape
    rows = normed_ref.shape[0]
    table = row_table(parts_ref.at[:, rows:total_rows, :], width)
    scale = jnp.broadcast_to(table[:, 127:128], (rows, 128))
    for part in range(parts):
        offset = jnp.broadcast_to(table[:, part : part + 1], (rows, 128))
        for start in range(0, width, 128):
            columns = slice(part * width + start, part * width + start + 128)
            values = parts_ref[part, :rows, start : start + 128].astype(F32)
            gain = 1.0 + mod_ref[1:2, columns]
            normed_ref[:, columns] = (
                ((values + offset) * scale) * gain + mod_ref[0:1, columns]
            ).astype(BF16)


def qkv_rows(parts_ref, mod_ref, weight_ref, normed_ref, held_ref=None, done=None):
    copies = []
    if held_ref is not None:
        copies = [
            pltpu.make_async_copy(weight_ref.at[which], held_ref.at[which], done.at[which])
            for which in range(3)
        ]
        for copy in copies:
            copy.start()
        weight_ref = held_ref
    modulate(parts_ref, mod_ref, normed_ref)
    rows = normed_ref.shape[0]
    tile = ROW_TILE if rows % ROW_TILE == 0 else rows
    for which in range(3):
        if copies:
            copies[which].wait()
        for start in range(0, rows, tile):
            span = slice(start, start + tile)
            yield which, span, jnp.dot(
                normed_ref[span, :], weight_ref[which], preferred_element_type=F32
            )


def space_in_kernel(parts_ref, mod_ref, weight_ref, q_ref, kv_ref, *scratch):
    for which, span, values in qkv_rows(parts_ref, mod_ref, weight_ref, *scratch):
        if which == 0:
            q_ref[span, :] = values.astype(BF16)
        else:
            kv_ref[which - 1, span, :] = values.astype(BF16)


def space_in(parts, mod, weight, rows):
    heads_width = weight.shape[2]
    return pl.pallas_call(
        space_in_kernel,
        in_specs=vmem(2) + [pl.BlockSpec(memory_space=pl.ANY)],
        out_specs=vmem(2),
        out_shape=[
            jax.ShapeDtypeStruct((rows, heads_width), BF16),
            jax.ShapeDtypeStruct((2, rows, heads_width), BF16),
        ],
        scratch_shapes=[
            pltpu.VMEM((rows, weight.shape[1]), BF16),
            pltpu.VMEM(weight.shape, BF16),
            pltpu.SemaphoreType.DMA((3,)),
        ],
        compiler_params=params(HELD_LIMIT),
        cost_estimate=pl.CostEstimate(
            flops=2 * rows * weight.size,
            bytes_accessed=2 * (weight.size + parts.size),
            transcendentals=0,
        ),
        name="space_in",
    )(parts, mod, weight)


def soft(scores):
    lifted = [jnp.exp(entry - jnp.max(entry, axis=1, keepdims=True)) for entry in scores]
    norms = [jnp.sum(entry, axis=1, keepdims=True) for entry in lifted]
    return [entry.astype(BF16) for entry in lifted], norms


def against(query, keys):
    return lax.dot_general(query, keys, (((1,), (1,)), ((), ())), preferred_element_type=F32)


def space_attend_kernel(where_ref, mask_ref, q_ref, own_ref, other_ref, out_ref):
    rows, heads_width = q_ref.shape
    query_blocks = rows // BLOCK
    key_blocks = 2 * query_blocks
    half = where_ref[1]
    mask_base = (where_ref[0] * key_blocks + half * query_blocks) * key_blocks
    biases = []
    for block in range(query_blocks):
        line = []
        for side in range(2):
            first = (half if side == 0 else 1 - half) * query_blocks
            for key_block in range(query_blocks):
                kept = mask_ref[mask_base + block * key_blocks + first + key_block]
                line.append(jnp.where(kept == 1, 0.0, -jnp.inf).astype(F32))
        biases.append(line)
    heads = [slice(start, start + HD) for start in range(0, heads_width, HD)]
    keys = [jnp.concatenate([own_ref[0, :, head], other_ref[0, :, head]], axis=0) for head in heads]
    values = [jnp.concatenate([own_ref[1, :, head], other_ref[1, :, head]], axis=0) for head in heads]
    units = [(head, block) for head in range(len(heads)) for block in range(query_blocks)]
    scores = [
        against(q_ref[block * BLOCK : (block + 1) * BLOCK, heads[head]], keys[head])
        for head, block in units
    ]
    scores = [
        jnp.concatenate(
            [
                entry[:, index * BLOCK : (index + 1) * BLOCK] * SCALE + bias
                for index, bias in enumerate(biases[block])
            ],
            axis=1,
        )
        for (_, block), entry in zip(units, scores)
    ]
    lifted, norms = soft(scores)
    for (head, block), entry, norm in zip(units, lifted, norms):
        mixed = jnp.dot(entry, values[head], preferred_element_type=F32) / norm
        out_ref[block * BLOCK : (block + 1) * BLOCK, heads[head]] = mixed.astype(BF16)


def space_attend(where, mask, queries, own, other):
    rows, heads_width = queries.shape
    return pl.pallas_call(
        space_attend_kernel,
        in_specs=smem(2) + vmem(3),
        out_specs=vmem(1)[0],
        out_shape=jax.ShapeDtypeStruct((rows, heads_width), BF16),
        compiler_params=params(),
        cost_estimate=pl.CostEstimate(
            flops=8 * rows * rows * heads_width,
            bytes_accessed=12 * rows * heads_width,
            transcendentals=2 * rows * rows * heads_width // HD,
        ),
        name="space_attend",
    )(where, mask, queries, own, other)


def lend_kernel(where_ref, *refs):
    layers = (len(refs) - 1) // 3
    done = refs[-1]
    side = where_ref[2] % 2
    copies = []
    for layer in range(layers):
        weight_ref, lent_ref, kept_ref = refs[layer], refs[layers + layer], refs[2 * layers + layer]
        groups, count, width = lent_ref.shape
        lines = pl.ds(pl.multiple_of(where_ref[1] * count, 128), count)
        for group in range(groups):
            there = pl.ds(pl.multiple_of((2 * group + 1 - side) * width, 128), width)
            here = pl.ds(pl.multiple_of((2 * group + side) * width, 128), width)
            copies.append((weight_ref.at[lines, there], lent_ref.at[group]))
            copies.append((weight_ref.at[:, here], kept_ref.at[group]))
    copies = [
        pltpu.make_async_copy(source, target, done.at[index])
        for index, (source, target) in enumerate(copies)
    ]
    for copy in copies:
        copy.start()
    for copy in copies:
        copy.wait()


def lend(where, weights, width):
    layers = len(weights)
    heads_width, model_width = weights[0].shape
    groups = model_width // (2 * width)
    lent = jax.ShapeDtypeStruct((groups, heads_width // 2, width), BF16)
    kept = jax.ShapeDtypeStruct((groups, heads_width, width), BF16)
    outs = pl.pallas_call(
        lend_kernel,
        in_specs=smem(1) + [pl.BlockSpec(memory_space=pl.ANY)] * layers,
        out_specs=vmem(2 * layers),
        out_shape=[lent] * layers + [kept] * layers,
        scratch_shapes=[pltpu.SemaphoreType.DMA((2 * groups * layers,))],
        compiler_params=params(),
        cost_estimate=pl.CostEstimate(
            flops=0, bytes_accessed=3 * layers * weights[0].size, transcendentals=0
        ),
        name="lend",
    )(where, *weights)
    return outs[:layers], outs[layers:]


def project_kernel(where_ref, own_ref, partner_ref, weight_ref, half_ref, other_half_ref, out_ref, lent_ref):
    groups = out_ref.shape[0]
    count = half_ref.shape[1]
    core = where_ref[1]
    lent_ref[:, pl.ds(pl.multiple_of(core * count, 128), count), :] = half_ref[...]
    lent_ref[:, pl.ds(pl.multiple_of((1 - core) * count, 128), count), :] = other_half_ref[...]
    for group in range(groups):
        product = jnp.dot(own_ref[...], weight_ref[group], preferred_element_type=F32)
        product += jnp.dot(partner_ref[...], lent_ref[group], preferred_element_type=F32)
        out_ref[group] = product.astype(BF16)


def project(where, own, partner, weight, half, other_half):
    rows, heads_width = own.shape
    groups, _, width = half.shape
    return pl.pallas_call(
        project_kernel,
        in_specs=smem(1) + vmem(5),
        out_specs=vmem(1)[0],
        out_shape=jax.ShapeDtypeStruct((groups, rows, width), BF16),
        scratch_shapes=[pltpu.VMEM((groups, heads_width, width), BF16)],
        compiler_params=params(),
        cost_estimate=pl.CostEstimate(
            flops=4 * rows * heads_width * groups * width,
            bytes_accessed=2 * groups * width * (rows + 2 * heads_width),
            transcendentals=0,
        ),
        name="project",
    )(where, own, partner, weight, half, other_half)


def local_gate(where_ref, mod_ref, width):
    return mod_ref[2:3, pl.ds(pl.multiple_of(where_ref[2] * width, 128), width)]


def join_kernel(where_ref, parts_ref, tokens_ref, mod_ref, stream_ref, *sent_refs):
    total = parts_ref[0].astype(F32)
    for part in range(1, parts_ref.shape[0]):
        total += parts_ref[part].astype(F32)
    stream = tokens_ref[...] + local_gate(where_ref, mod_ref, total.shape[1]) * total
    stream_ref[...] = stream
    for sent_ref in sent_refs:
        sent_ref[...] = stream.astype(BF16)


def join(where, parts, tokens, mod, dtypes):
    count, rows, width = parts.shape
    return pl.pallas_call(
        join_kernel,
        in_specs=smem(1) + vmem(3),
        out_specs=vmem(len(dtypes)),
        out_shape=[jax.ShapeDtypeStruct((rows, width), dtype) for dtype in dtypes],
        compiler_params=params(),
        name="join",
    )(where, parts, tokens, mod)


def time_kernel(parts_ref, mod_ref, weight_ref, out_ref, packed_ref, att_ref, *scratch):
    frames, places, heads_width = att_ref.shape
    for which, span, values in qkv_rows(parts_ref, mod_ref, weight_ref, *scratch):
        first = span.start // places
        count = values.shape[0] // places
        packed_ref[which, first : first + count] = values.reshape(count, places, heads_width)
    group = 8
    span = frames * group
    row_place = lax.broadcasted_iota(jnp.int32, (span, span), 0) % group
    col_place = lax.broadcasted_iota(jnp.int32, (span, span), 1) % group
    bias = jnp.where(row_place == col_place, 0.0, -jnp.inf).astype(F32)
    units = [(start, low) for start in range(0, places, group) for low in range(0, heads_width, HD)]

    def chosen(which, start, low):
        block = packed_ref[which, :, start : start + group, low : low + HD]
        return block.reshape(span, HD).astype(BF16)

    scores = [against(chosen(0, *unit), chosen(1, *unit)) * SCALE + bias for unit in units]
    lifted, norms = soft(scores)
    for unit, entry, norm in zip(units, lifted, norms):
        mixed = jnp.dot(entry, chosen(2, *unit), preferred_element_type=F32) / norm
        start, low = unit
        att_ref[:, start : start + group, low : low + HD] = mixed.reshape(frames, group, HD)
    out_ref[...] = att_ref[...].reshape(frames * places, heads_width).astype(BF16)


def time_layer(parts, mod, weight, rows, frames):
    heads_width = weight.shape[2]
    return pl.pallas_call(
        time_kernel,
        in_specs=vmem(3),
        out_specs=vmem(1)[0],
        out_shape=jax.ShapeDtypeStruct((rows, heads_width), BF16),
        scratch_shapes=[
            pltpu.VMEM((3, frames, rows // frames, heads_width), F32),
            pltpu.VMEM((frames, rows // frames, heads_width), F32),
            pltpu.VMEM((rows, weight.shape[1]), BF16),
        ],
        compiler_params=params(),
        cost_estimate=pl.CostEstimate(
            flops=2 * rows * weight.size,
            bytes_accessed=2 * (weight.size + parts.size),
            transcendentals=rows * BLOCK * heads_width // HD,
        ),
        name="time_layer",
    )(parts, mod, weight)


def on_device(tokens, block_mask, space_qkv, space_out, space_mod, time_qkv, time_out, time_mod):
    videos, rows, width = tokens.shape
    parts = lax.axis_size("fsdp")
    seq_count = lax.axis_size("seq")
    frames = seq_count // 2
    seq_index = lax.axis_index("seq")
    where = jnp.stack([seq_index // 2, seq_index % 2, lax.axis_index("fsdp")]).astype(jnp.int32)
    same_half = [[2 * frame + half for frame in range(frames)] for half in range(2)]

    def across_frames(values):
        return lax.all_to_all(
            values.reshape(frames, rows // frames, -1), "seq", split_axis=0, concat_axis=0,
            tiled=True, axis_index_groups=same_half,
        ).reshape(rows, -1)

    def across_parts(values):
        return lax.all_to_all(values, "fsdp", split_axis=0, concat_axis=0, tiled=True)

    def gathered(shard):
        return across_parts(jnp.broadcast_to(shard[None], (parts,) + shard.shape))

    def from_other_core(values):
        return lax.ppermute(values, "seq", [(i, i ^ 1) for i in range(seq_count)])

    def from_other_side(values):
        return lax.ppermute(values, "fsdp", [(i, i ^ 1) for i in range(parts)])

    def projected(attended, weight, half):
        return project(
            where, attended, from_other_side(attended), weight, half, from_other_core(half)
        )

    def across_x(values):
        same_side = [[2 * group + side for group in range(parts // 2)] for side in range(2)]
        return lax.all_to_all(
            values, "fsdp", split_axis=0, concat_axis=0, tiled=True, axis_index_groups=same_side
        )

    local = tokens.reshape(rows, width)
    (space_lent, time_lent), (space_kept, time_kept) = lend(where, (space_out, time_out), width)
    half = from_other_side(space_lent)
    queries, own = space_in(gathered(pack(local)), space_mod, jnp.swapaxes(space_qkv, 0, 1), rows)
    attended = space_attend(where, block_mask.reshape(-1), queries, own, from_other_core(own))
    partial = projected(attended, space_kept, half)
    partial, time_lent = lax.optimization_barrier((partial, time_lent))
    half = from_other_side(time_lent)
    stream, sent = join(where, across_x(partial), local, space_mod, (F32, BF16))
    sent, half = lax.optimization_barrier((sent, half))
    wide = gathered(pack(across_frames(sent)))
    attended = time_layer(wide, time_mod, jnp.swapaxes(time_qkv, 0, 1), rows, frames)
    arrived = across_x(projected(across_frames(attended), time_kept, half))
    return join(where, arrived, stream, time_mod, (F32,))[0].reshape(tokens.shape)


def solution(mesh):
    placed = (
        P(None, "seq", "fsdp"),
        P(),
        P(None, None, "fsdp"),
        P("fsdp", None),
        P(),
        P(None, None, "fsdp"),
        P("fsdp", None),
        P(),
    )
    return jax.shard_map(
        on_device, mesh=mesh, in_specs=placed, out_specs=P(None, "seq", "fsdp"), check_vma=False
    )
```

```python
import functools
import math

import jax
import jax.numpy as jnp
from jax import lax
from jax.experimental import pallas as pl
from jax.experimental.pallas import tpu as pltpu
from jax.sharding import PartitionSpec as P

HD = 128
BLOCK = 128
EPS = 1e-06
SCALE = 1.0 / math.sqrt(HD)
VMEM_LIMIT = 24 * 1024 * 1024
HELD_LIMIT = 50 * 1024 * 1024
ROW_TILE = 192
F32 = jnp.float32
BF16 = jnp.bfloat16
STAT_ROWS = 8


def vmem(count):
    return [pl.BlockSpec(memory_space=pltpu.VMEM)] * count


def smem(count):
    return [pl.BlockSpec(memory_space=pltpu.SMEM)] * count


def params(limit=None):
    return pltpu.CompilerParams(vmem_limit_bytes=limit or VMEM_LIMIT)


def spread_columns(columns, rows):
    lane = lax.broadcasted_iota(jnp.int32, (rows, 128), 1)
    table = jnp.zeros((rows, 128), F32)
    for index, column in enumerate(columns):
        table = jnp.where(lane == index, column, table)
    return table


def bf16_terms(values, count):
    terms = []
    for _ in range(count):
        term = values.astype(BF16).astype(F32)
        terms.append(term)
        values = values - term
    return terms


def centre(values):
    mean = jnp.sum(values, axis=1, keepdims=True) / values.shape[1]
    centred = values - mean
    squares = jnp.sum(centred * centred, axis=1, keepdims=True)
    table = spread_columns(bf16_terms(mean, 3) + bf16_terms(squares, 2), values.shape[0])
    return centred.astype(BF16), table


def pack_kernel(tokens_ref, out_ref):
    rows = tokens_ref.shape[0]
    centred, table = centre(tokens_ref[...].astype(F32))
    out_ref[:rows, :] = centred
    out_ref[rows:, :] = jnp.transpose(table)[:STAT_ROWS].astype(BF16)


def pack(tokens):
    rows, width = tokens.shape
    shape = (rows + STAT_ROWS, width)
    return pl.pallas_call(
        pack_kernel,
        in_specs=vmem(1),
        out_specs=vmem(1)[0],
        out_shape=jax.ShapeDtypeStruct(shape, BF16),
        compiler_params=params(),
        name="pack",
    )(tokens)


def row_table(stats_ref, width):
    parts, _, rows = stats_ref.shape
    line = lax.broadcasted_iota(jnp.int32, (parts, rows), 0)
    means = jnp.zeros((parts, rows), F32)
    squares = 0.0
    for part in range(parts):
        lines = stats_ref[part].astype(F32)
        means = jnp.where(line == part, lines[0:1] + lines[1:2] + lines[2:3], means)
        squares = squares + (lines[3:4] + lines[4:5])
    offsets = means - jnp.sum(means, axis=0, keepdims=True) / parts
    between = jnp.sum(offsets * offsets, axis=0, keepdims=True) * width
    scale = lax.rsqrt((squares + between) / (parts * width) + EPS)
    scales = jnp.broadcast_to(scale, (128 - parts, rows))
    return jnp.transpose(jnp.concatenate([offsets, scales], axis=0))


def modulate(parts_ref, mod_ref, normed_ref):
    parts, total_rows, width = parts_ref.shape
    rows = normed_ref.shape[0]
    table = row_table(parts_ref.at[:, rows:total_rows, :], width)
    scale = jnp.broadcast_to(table[:, 127:128], (rows, 128))
    for part in range(parts):
        offset = jnp.broadcast_to(table[:, part : part + 1], (rows, 128))
        for start in range(0, width, 128):
            columns = slice(part * width + start, part * width + start + 128)
            values = parts_ref[part, :rows, start : start + 128].astype(F32)
            gain = 1.0 + mod_ref[1:2, columns]
            normed_ref[:, columns] = (
                ((values + offset) * scale) * gain + mod_ref[0:1, columns]
            ).astype(BF16)


def qkv_rows(parts_ref, mod_ref, weight_ref, normed_ref, held_ref=None, done=None):
    copies = []
    if held_ref is not None:
        copies = [
            pltpu.make_async_copy(weight_ref.at[which], held_ref.at[which], done.at[which])
            for which in range(3)
        ]
        for copy in copies:
            copy.start()
        weight_ref = held_ref
    modulate(parts_ref, mod_ref, normed_ref)
    rows = normed_ref.shape[0]
    tile = ROW_TILE if rows % ROW_TILE == 0 else rows
    for which in range(3):
        if copies:
            copies[which].wait()
        for start in range(0, rows, tile):
            span = slice(start, start + tile)
            yield which, span, jnp.dot(
                normed_ref[span, :], weight_ref[which], preferred_element_type=F32
            )


def space_in_kernel(parts_ref, mod_ref, weight_ref, q_ref, kv_ref, *scratch):
    for which, span, values in qkv_rows(parts_ref, mod_ref, weight_ref, *scratch):
        if which == 0:
            q_ref[span, :] = values.astype(BF16)
        else:
            kv_ref[which - 1, span, :] = values.astype(BF16)


def space_in(parts, mod, weight, rows):
    heads_width = weight.shape[2]
    return pl.pallas_call(
        space_in_kernel,
        in_specs=vmem(2) + [pl.BlockSpec(memory_space=pl.ANY)],
        out_specs=vmem(2),
        out_shape=[
            jax.ShapeDtypeStruct((rows, heads_width), BF16),
            jax.ShapeDtypeStruct((2, rows, heads_width), BF16),
        ],
        scratch_shapes=[
            pltpu.VMEM((rows, weight.shape[1]), BF16),
            pltpu.VMEM(weight.shape, BF16),
            pltpu.SemaphoreType.DMA((3,)),
        ],
        compiler_params=params(HELD_LIMIT),
        cost_estimate=pl.CostEstimate(
            flops=2 * rows * weight.size,
            bytes_accessed=2 * (weight.size + parts.size),
            transcendentals=0,
        ),
        name="space_in",
    )(parts, mod, weight)


def soft(scores):
    lifted = [jnp.exp(entry - jnp.max(entry, axis=1, keepdims=True)) for entry in scores]
    norms = [jnp.sum(entry, axis=1, keepdims=True) for entry in lifted]
    return [entry.astype(BF16) for entry in lifted], norms


def against(query, keys):
    return lax.dot_general(query, keys, (((1,), (1,)), ((), ())), preferred_element_type=F32)


def space_attend_kernel(where_ref, mask_ref, q_ref, own_ref, other_ref, out_ref):
    rows, heads_width = q_ref.shape
    query_blocks = rows // BLOCK
    key_blocks = 2 * query_blocks
    half = where_ref[1]
    mask_base = (where_ref[0] * key_blocks + half * query_blocks) * key_blocks
    biases = []
    for block in range(query_blocks):
        line = []
        for side in range(2):
            first = (half if side == 0 else 1 - half) * query_blocks
            for key_block in range(query_blocks):
                kept = mask_ref[mask_base + block * key_blocks + first + key_block]
                line.append(jnp.where(kept == 1, 0.0, -jnp.inf).astype(F32))
        biases.append(line)
    heads = [slice(start, start + HD) for start in range(0, heads_width, HD)]
    keys = [jnp.concatenate([own_ref[0, :, head], other_ref[0, :, head]], axis=0) for head in heads]
    values = [jnp.concatenate([own_ref[1, :, head], other_ref[1, :, head]], axis=0) for head in heads]
    units = [(head, block) for head in range(len(heads)) for block in range(query_blocks)]
    scores = [
        against(q_ref[block * BLOCK : (block + 1) * BLOCK, heads[head]], keys[head])
        for head, block in units
    ]
    scores = [
        jnp.concatenate(
            [
                entry[:, index * BLOCK : (index + 1) * BLOCK] * SCALE + bias
                for index, bias in enumerate(biases[block])
            ],
            axis=1,
        )
        for (_, block), entry in zip(units, scores)
    ]
    lifted, norms = soft(scores)
    for (head, block), entry, norm in zip(units, lifted, norms):
        mixed = jnp.dot(entry, values[head], preferred_element_type=F32) / norm
        out_ref[block * BLOCK : (block + 1) * BLOCK, heads[head]] = mixed.astype(BF16)


def space_attend(where, mask, queries, own, other):
    rows, heads_width = queries.shape
    return pl.pallas_call(
        space_attend_kernel,
        in_specs=smem(2) + vmem(3),
        out_specs=vmem(1)[0],
        out_shape=jax.ShapeDtypeStruct((rows, heads_width), BF16),
        compiler_params=params(),
        cost_estimate=pl.CostEstimate(
            flops=8 * rows * rows * heads_width,
            bytes_accessed=12 * rows * heads_width,
            transcendentals=2 * rows * rows * heads_width // HD,
        ),
        name="space_attend",
    )(where, mask, queries, own, other)


def lend_kernel(where_ref, *refs):
    layers = (len(refs) - 1) // 3
    done = refs[-1]
    side = where_ref[2] % 2
    copies = []
    for layer in range(layers):
        weight_ref, lent_ref, kept_ref = refs[layer], refs[layers + layer], refs[2 * layers + layer]
        groups, count, width = lent_ref.shape
        lines = pl.ds(pl.multiple_of(where_ref[1] * count, 128), count)
        for group in range(groups):
            there = pl.ds(pl.multiple_of((2 * group + 1 - side) * width, 128), width)
            here = pl.ds(pl.multiple_of((2 * group + side) * width, 128), width)
            copies.append((weight_ref.at[lines, there], lent_ref.at[group]))
            copies.append((weight_ref.at[:, here], kept_ref.at[group]))
    copies = [
        pltpu.make_async_copy(source, target, done.at[index])
        for index, (source, target) in enumerate(copies)
    ]
    for copy in copies:
        copy.start()
    for copy in copies:
        copy.wait()


def lend(where, weights, width):
    layers = len(weights)
    heads_width, model_width = weights[0].shape
    groups = model_width // (2 * width)
    lent = jax.ShapeDtypeStruct((groups, heads_width // 2, width), BF16)
    kept = jax.ShapeDtypeStruct((groups, heads_width, width), BF16)
    outs = pl.pallas_call(
        lend_kernel,
        in_specs=smem(1) + [pl.BlockSpec(memory_space=pl.ANY)] * layers,
        out_specs=vmem(2 * layers),
        out_shape=[lent] * layers + [kept] * layers,
        scratch_shapes=[pltpu.SemaphoreType.DMA((2 * groups * layers,))],
        compiler_params=params(),
        cost_estimate=pl.CostEstimate(
            flops=0, bytes_accessed=3 * layers * weights[0].size, transcendentals=0
        ),
        name="lend",
    )(where, *weights)
    return outs[:layers], outs[layers:]


def project_kernel(where_ref, own_ref, partner_ref, weight_ref, half_ref, other_half_ref, out_ref, lent_ref):
    groups = out_ref.shape[0]
    count = half_ref.shape[1]
    core = where_ref[1]
    lent_ref[:, pl.ds(pl.multiple_of(core * count, 128), count), :] = half_ref[...]
    lent_ref[:, pl.ds(pl.multiple_of((1 - core) * count, 128), count), :] = other_half_ref[...]
    for group in range(groups):
        product = jnp.dot(own_ref[...], weight_ref[group], preferred_element_type=F32)
        product += jnp.dot(partner_ref[...], lent_ref[group], preferred_element_type=F32)
        out_ref[group] = product.astype(BF16)


def project(where, own, partner, weight, half, other_half):
    rows, heads_width = own.shape
    groups, _, width = half.shape
    return pl.pallas_call(
        project_kernel,
        in_specs=smem(1) + vmem(5),
        out_specs=vmem(1)[0],
        out_shape=jax.ShapeDtypeStruct((groups, rows, width), BF16),
        scratch_shapes=[pltpu.VMEM((groups, heads_width, width), BF16)],
        compiler_params=params(),
        cost_estimate=pl.CostEstimate(
            flops=4 * rows * heads_width * groups * width,
            bytes_accessed=2 * groups * width * (rows + 2 * heads_width),
            transcendentals=0,
        ),
        name="project",
    )(where, own, partner, weight, half, other_half)


def local_gate(where_ref, mod_ref, width):
    return mod_ref[2:3, pl.ds(pl.multiple_of(where_ref[2] * width, 128), width)]


def join_kernel(where_ref, parts_ref, tokens_ref, mod_ref, stream_ref, *sent_refs):
    total = parts_ref[0].astype(F32)
    for part in range(1, parts_ref.shape[0]):
        total += parts_ref[part].astype(F32)
    stream = tokens_ref[...] + local_gate(where_ref, mod_ref, total.shape[1]) * total
    stream_ref[...] = stream
    for sent_ref in sent_refs:
        sent_ref[...] = stream.astype(BF16)


def join(where, parts, tokens, mod, dtypes):
    count, rows, width = parts.shape
    return pl.pallas_call(
        join_kernel,
        in_specs=smem(1) + vmem(3),
        out_specs=vmem(len(dtypes)),
        out_shape=[jax.ShapeDtypeStruct((rows, width), dtype) for dtype in dtypes],
        compiler_params=params(),
        name="join",
    )(where, parts, tokens, mod)


def time_kernel(parts_ref, mod_ref, weight_ref, out_ref, packed_ref, att_ref, *scratch):
    frames, places, heads_width = att_ref.shape
    for which, span, values in qkv_rows(parts_ref, mod_ref, weight_ref, *scratch):
        first = span.start // places
        count = values.shape[0] // places
        packed_ref[which, first : first + count] = values.reshape(count, places, heads_width)
    group = 8
    span = frames * group
    row_place = lax.broadcasted_iota(jnp.int32, (span, span), 0) % group
    col_place = lax.broadcasted_iota(jnp.int32, (span, span), 1) % group
    bias = jnp.where(row_place == col_place, 0.0, -jnp.inf).astype(F32)
    units = [(start, low) for start in range(0, places, group) for low in range(0, heads_width, HD)]

    def chosen(which, start, low):
        block = packed_ref[which, :, start : start + group, low : low + HD]
        return block.reshape(span, HD).astype(BF16)

    scores = [against(chosen(0, *unit), chosen(1, *unit)) * SCALE + bias for unit in units]
    lifted, norms = soft(scores)
    for unit, entry, norm in zip(units, lifted, norms):
        mixed = jnp.dot(entry, chosen(2, *unit), preferred_element_type=F32) / norm
        start, low = unit
        att_ref[:, start : start + group, low : low + HD] = mixed.reshape(frames, group, HD)
    out_ref[...] = att_ref[...].reshape(frames * places, heads_width).astype(BF16)


def time_layer(parts, mod, weight, rows, frames):
    heads_width = weight.shape[2]
    return pl.pallas_call(
        time_kernel,
        in_specs=vmem(3),
        out_specs=vmem(1)[0],
        out_shape=jax.ShapeDtypeStruct((rows, heads_width), BF16),
        scratch_shapes=[
            pltpu.VMEM((3, frames, rows // frames, heads_width), F32),
            pltpu.VMEM((frames, rows // frames, heads_width), F32),
            pltpu.VMEM((rows, weight.shape[1]), BF16),
        ],
        compiler_params=params(),
        cost_estimate=pl.CostEstimate(
            flops=2 * rows * weight.size,
            bytes_accessed=2 * (weight.size + parts.size),
            transcendentals=rows * BLOCK * heads_width // HD,
        ),
        name="time_layer",
    )(parts, mod, weight)


def on_device(tokens, block_mask, space_qkv, space_out, space_mod, time_qkv, time_out, time_mod):
    videos, rows, width = tokens.shape
    parts = lax.axis_size("fsdp")
    seq_count = lax.axis_size("seq")
    frames = seq_count // 2
    seq_index = lax.axis_index("seq")
    where = jnp.stack([seq_index // 2, seq_index % 2, lax.axis_index("fsdp")]).astype(jnp.int32)
    same_half = [[2 * frame + half for frame in range(frames)] for half in range(2)]

    def across_frames(values):
        return lax.all_to_all(
            values.reshape(frames, rows // frames, -1), "seq", split_axis=0, concat_axis=0,
            tiled=True, axis_index_groups=same_half,
        ).reshape(rows, -1)

    def across_parts(values):
        return lax.all_to_all(values, "fsdp", split_axis=0, concat_axis=0, tiled=True)

    def gathered(shard):
        return across_parts(jnp.broadcast_to(shard[None], (parts,) + shard.shape))

    def from_other_core(values):
        return lax.ppermute(values, "seq", [(i, i ^ 1) for i in range(seq_count)])

    def from_other_side(values):
        return lax.ppermute(values, "fsdp", [(i, i ^ 1) for i in range(parts)])

    def projected(attended, weight, half):
        return project(
            where, attended, from_other_side(attended), weight, half, from_other_core(half)
        )

    def across_x(values):
        same_side = [[2 * group + side for group in range(parts // 2)] for side in range(2)]
        return lax.all_to_all(
            values, "fsdp", split_axis=0, concat_axis=0, tiled=True, axis_index_groups=same_side
        )

    local = tokens.reshape(rows, width)
    (space_lent, time_lent), (space_kept, time_kept) = lend(where, (space_out, time_out), width)
    half = from_other_side(space_lent)
    queries, own = space_in(gathered(pack(local)), space_mod, jnp.swapaxes(space_qkv, 0, 1), rows)
    attended = space_attend(where, block_mask.reshape(-1), queries, own, from_other_core(own))
    partial = projected(attended, space_kept, half)
    partial, time_lent = lax.optimization_barrier((partial, time_lent))
    half = from_other_side(time_lent)
    stream, sent = join(where, across_x(partial), local, space_mod, (F32, BF16))
    sent, half = lax.optimization_barrier((sent, half))
    wide = gathered(pack(across_frames(sent)))
    attended = time_layer(wide, time_mod, jnp.swapaxes(time_qkv, 0, 1), rows, frames)
    arrived = across_x(projected(across_frames(attended), time_kept, half))
    return join(where, arrived, stream, time_mod, (F32,))[0].reshape(tokens.shape)


def solution(mesh):
    placed = (
        P(None, "seq", "fsdp"),
        P(),
        P(None, None, "fsdp"),
        P("fsdp", None),
        P(),
        P(None, None, "fsdp"),
        P("fsdp", None),
        P(),
    )
    return jax.shard_map(
        on_device, mesh=mesh, in_specs=placed, out_specs=P(None, "seq", "fsdp"), check_vma=False
    )
```
